32 devices in a mesh: dp: 8 (over y, x, core), mp: 4 (over z).
Axes of the slice: x: 2, y: 2, z: 4, core: 2. Of those that a mesh axis runs over, the one named last changes fastest.
Arguments:
- inputs: bfloat16 [8, 2048, 1024], P('dp', 'mp'), may hold values from -6 to 6
- cotangent: bfloat16 [8, 2048, 1024], P('dp', 'mp'), may hold values from -6 to 6
- segment_ids: int32 [8, 2048], P('dp'), may hold values from 0 to 2048, as said below
- row_length: int32 [8], P('dp'), may hold values from 1792 to 2048, as said below
- w_qkv: float32 [3, 1024, 1024], P(None, 'dp', 'mp'), may hold values from -0.09375 to 0.09375
- m_qkv: float32 [3, 1024, 1024], P(None, 'dp', 'mp'), may hold values from -320 to 320
- v_qkv: float32 [3, 1024, 1024], P(None, 'dp', 'mp'), may hold values from 131.072 to 2097.152
- w_out: float32 [1024, 1024], P('mp', 'dp'), may hold values from -1.5 to 1.5
- m_out: float32 [1024, 1024], P('mp', 'dp'), may hold values from -16 to 16
- v_out: float32 [1024, 1024], P('mp', 'dp'), may hold values from 0.2654208 to 4.25984
- w_gate_up: float32 [2, 1024, 2816], P(None, 'dp', 'mp'), may hold values from -0.1875 to 0.1875
- m_gate_up: float32 [2, 1024, 2816], P(None, 'dp', 'mp'), may hold values from -32 to 32
- v_gate_up: float32 [2, 1024, 2816], P(None, 'dp', 'mp'), may hold values from 1.122304 to 18.0224
- w_down: float32 [2816, 1024], P('mp', 'dp'), may hold values from -0.109375 to 0.109375
- m_down: float32 [2816, 1024], P('mp', 'dp'), may hold values from -56 to 56
- v_down: float32 [2816, 1024], P('mp', 'dp'), may hold values from 3.44064 to 55.7056
- norm_gains: float32 [2, 1024], P(None, 'dp'), may hold values from 0.5 to 1.5
- m_gains: float32 [2, 1024], P(None, 'dp'), may hold values from -128 to 128
- v_gains: float32 [2, 1024], P(None, 'dp'), may hold values from 16.384 to 262.144
Outputs:
- block_output: float32 [8, 2048, 1024], P('dp', 'mp')
- input_grad: float32 [8, 2048, 1024], P('dp', 'mp')
- qkv_new: float32 [3, 1024, 1024], P(None, 'dp', 'mp')
- qkv_copy: bfloat16 [3, 1024, 1024], P(None, 'dp', 'mp')
- qkv_moment: float32 [3, 1024, 1024], P(None, 'dp', 'mp')
- qkv_second: float32 [3, 1024, 1024], P(None, 'dp', 'mp')
- out_new: float32 [1024, 1024], P('mp', 'dp')
- out_copy: bfloat16 [1024, 1024], P('mp', 'dp')
- out_moment: float32 [1024, 1024], P('mp', 'dp')
- out_second: float32 [1024, 1024], P('mp', 'dp')
- gate_up_new: float32 [2, 1024, 2816], P(None, 'dp', 'mp')
- gate_up_copy: bfloat16 [2, 1024, 2816], P(None, 'dp', 'mp')
- gate_up_moment: float32 [2, 1024, 2816], P(None, 'dp', 'mp')
- gate_up_second: float32 [2, 1024, 2816], P(None, 'dp', 'mp')
- down_new: float32 [2816, 1024], P('mp', 'dp')
- down_copy: bfloat16 [2816, 1024], P('mp', 'dp')
- down_moment: float32 [2816, 1024], P('mp', 'dp')
- down_second: float32 [2816, 1024], P('mp', 'dp')
- gains_new: float32 [2, 1024], P(None, 'dp')
- gains_copy: bfloat16 [2, 1024], P(None, 'dp')
- gains_moment: float32 [2, 1024], P(None, 'dp')
- gains_second: float32 [2, 1024], P(None, 'dp')
The draws below stay inside these ranges and needn't reach their ends.
Inputs may be any that keep to these rules, and one draw needn't show every extreme that they name: A row's live tokens are its positions below row_length; some row is full and some holds exactly the least. `segment_ids`: ids never fall along a row; positions at or past the row's length hold 2048 and live ones less; each run of one id among live positions is one packed document.
All inputs are finite; a program needn't handle non-finite values.
Results may differ from the reference program's by a relative error of at most 0.019.
The reference program's roundings to bfloat16 on the way count: a program that leaves them out, or rounds other values in their place, can miss the bound.
Values may be sent and summed in bfloat16 or wider, within the bound.
No kernel may reach another device: no remote copies, remote signals or barrier semaphores. Data moves between devices by JAX's collectives and lax.ppermute only.
A program may use at most 192 MiB of HBM per device.

```python
import math
import jax
import jax.numpy as jnp
from jax import lax

D = 1024
HEADS = 16
HEAD = 64
FF = 2816
SEQ = 2048
ADAM_STEP = 5
ROWS = 8


def packing(key):
    length_key = jax.random.fold_in(key, 11)
    boundary_key = jax.random.fold_in(key, 12)
    shortest = SEQ - SEQ // 8
    row_lengths = jax.random.randint(length_key, (ROWS,), shortest, SEQ + 1)
    row_lengths = row_lengths.at[0].set(SEQ).at[1].set(shortest)
    boundary = (jax.random.randint(boundary_key, (ROWS, SEQ), 0, SEQ // 4) == 0).astype(jnp.int32)
    boundary = boundary.at[:, 0].set(0)
    segment = jnp.cumsum(boundary, axis=1)
    positions = jnp.arange(SEQ, dtype=jnp.int32)[None, :]
    segment = jnp.where(positions < row_lengths[:, None], segment, SEQ)
    return (row_lengths.astype(jnp.int32), segment.astype(jnp.int32))


def draw_row_length(key, part):
    return packing(key)[0]


def draw_segment_ids(key, part):
    return packing(key)[1]


def levels(key, extent, cuts, low, largest):
    def one(position, blocks):
        heights = jax.random.uniform(jax.random.fold_in(jax.random.fold_in(key, 6), position), (blocks,), jnp.float32, low / len(cuts), largest / len(cuts))
        return jnp.repeat(jnp.exp(heights), extent[position] // blocks).reshape((-1,) + (1,) * (len(extent) - position - 1))

    level = one(*cuts[0])
    for cut in cuts[1:]:
        level = level * one(*cut)
    return level


def gaussian(key, dims, spread, most, shards=(), kind=jnp.bfloat16):
    result = spread * jax.random.normal(key, dims, jnp.float32)
    if shards:
        result = result * levels(key, dims, shards, -0.22, 0.18)
    return jnp.clip(result, -most, most).astype(kind)


def setup_inputs(seed: int = 0) -> dict:
    keys = jax.random.split(jax.random.key(seed), 20)
    inputs = gaussian(keys[0], (ROWS, SEQ, D), 1.0, 6.0, ((0, 8), (1, 4)))
    cotangent = gaussian(keys[1], (ROWS, SEQ, D), 1.0, 6.0, ((0, 8), (1, 4)))
    segment_ids = draw_segment_ids(jax.random.fold_in(keys[19], 71), 0)
    row_length = draw_row_length(jax.random.fold_in(keys[19], 71), 0)
    w_qkv = gaussian(keys[4], (3, D, HEADS * HEAD), (4 * D) ** -0.5, 0.09375, ((1, 8), (2, 4)), jnp.float32)
    m_qkv = gaussian(keys[5], (3, D, HEADS * HEAD), (0.44 * (ROWS * SEQ) ** 0.5), 320.0, ((1, 8), (2, 4)), jnp.float32)
    v_qkv = jnp.clip(jnp.exp(math.log(2097.152) - 2.7725887 * jax.random.uniform(keys[6], (3, D, HEADS * HEAD), jnp.float32) ** levels(keys[6], (3, D, HEADS * HEAD), ((1, 8), (2, 4)), -0.2, 0.2)), 131.072, 2097.152)
    w_out = gaussian(keys[7], (HEADS * HEAD, D), (HEADS * HEAD // 64) ** -0.5, 1.5, ((0, 4), (1, 8)), jnp.float32)
    m_out = gaussian(keys[8], (HEADS * HEAD, D), (0.02 * (ROWS * SEQ) ** 0.5), 16.0, ((0, 4), (1, 8)), jnp.float32)
    v_out = jnp.clip(jnp.exp(math.log(4.25984) - 2.77567041 * jax.random.uniform(keys[9], (HEADS * HEAD, D), jnp.float32) ** levels(keys[9], (HEADS * HEAD, D), ((0, 4), (1, 8)), -0.2, 0.2)), 0.2654208, 4.25984)
    w_gate_up = gaussian(keys[10], (2, D, FF), D ** -0.5, 0.1875, ((1, 8), (2, 4)), jnp.float32)
    m_gate_up = gaussian(keys[11], (2, D, FF), (0.041 * (ROWS * SEQ) ** 0.5), 32.0, ((1, 8), (2, 4)), jnp.float32)
    v_gate_up = jnp.clip(jnp.exp(math.log(18.0224) - 2.7762317 * jax.random.uniform(keys[12], (2, D, FF), jnp.float32) ** levels(keys[12], (2, D, FF), ((1, 8), (2, 4)), -0.2, 0.2)), 1.122304, 18.0224)
    w_down = gaussian(keys[13], (FF, D), FF ** -0.5, 0.109375, ((0, 4), (1, 8)), jnp.float32)
    m_down = gaussian(keys[14], (FF, D), (0.072 * (ROWS * SEQ) ** 0.5), 56.0, ((0, 4), (1, 8)), jnp.float32)
    v_down = jnp.clip(jnp.exp(math.log(55.7056) - 2.784423 * jax.random.uniform(keys[15], (FF, D), jnp.float32) ** levels(keys[15], (FF, D), ((0, 4), (1, 8)), -0.2, 0.2)), 3.44064, 55.7056)
    norm_gains = jnp.clip(1.0 + 0.1 * jax.random.normal(keys[16], (2, D), jnp.float32), 0.5, 1.5)
    m_gains = gaussian(keys[17], (2, D), (0.155 * (ROWS * SEQ) ** 0.5), 128.0, ((1, 8),), jnp.float32)
    v_gains = jnp.clip(jnp.exp(math.log(262.144) - 2.7725887 * jax.random.uniform(keys[18], (2, D), jnp.float32) ** levels(keys[18], (2, D), ((1, 8),), -0.2, 0.2)), 16.384, 262.144)
    return {"inputs": inputs, "cotangent": cotangent, "segment_ids": segment_ids, "row_length": row_length, "w_qkv": w_qkv, "m_qkv": m_qkv, "v_qkv": v_qkv, "w_out": w_out, "m_out": m_out, "v_out": v_out, "w_gate_up": w_gate_up, "m_gate_up": m_gate_up, "v_gate_up": v_gate_up, "w_down": w_down, "m_down": m_down, "v_down": v_down, "norm_gains": norm_gains, "m_gains": m_gains, "v_gains": v_gains}


EPS_NORM = 1e-06
BETA_ONE = 0.9
BETA_TWO = 0.999
ADAM_EPS = 1e-08
DECAY_RATE = 0.1
RATES = (0.03, 0.5, 0.06, 0.04, 0.4)
NEG_FILL = -1e+30

@jax.custom_vjp
def low(v):
    return lax.optimization_barrier(v.astype(jnp.bfloat16)).astype(jnp.float32)

@jax.custom_vjp
def low_back(v):
    return v

def low_keep(v):
    return (low(v), None)

def low_pass(kept, grad):
    return (grad,)

def back_keep(v):
    return (v, None)

def back_low(kept, grad):
    return (low(grad),)
low.defvjp(low_keep, low_pass)
low_back.defvjp(back_keep, back_low)

def product(left, right):
    return jnp.dot(left, right, precision=lax.Precision.HIGHEST, preferred_element_type=jnp.float32)

def rms_norm(values_in, gain):
    scale = lax.rsqrt(lax.optimization_barrier(jnp.mean(values_in * values_in, axis=-1, keepdims=True)) + EPS_NORM)
    return values_in * scale * gain

def row_forward(weights, row_in, seg_row, live_row):
    full_qkv, full_out, full_gate_up, full_down, full_gains = weights
    normed_one = low(rms_norm(row_in, full_gains[0]))
    queries = low_back(low(product(normed_one, full_qkv[0]))).reshape(SEQ, HEADS, HEAD)
    keys_all = low_back(low(product(normed_one, full_qkv[1]))).reshape(SEQ, HEADS, HEAD)
    values_all = low_back(low(product(normed_one, full_qkv[2]))).reshape(SEQ, HEADS, HEAD)
    block_rows = min(512, SEQ)
    blocks = SEQ // block_rows

    def attend(block_in):
        query_blk, seg_blk = block_in
        scores = jnp.einsum('qhd,khd->hqk', query_blk, keys_all, precision=lax.Precision.HIGHEST)
        scores = low_back(scores)
        same_doc = (seg_blk[:, None] == seg_row[None, :])[None]
        scores = jnp.where(same_doc, scores, NEG_FILL)
        row_peak = lax.optimization_barrier(jnp.max(scores, axis=-1, keepdims=True))
        raised = jnp.exp(scores - row_peak)
        probs = raised / lax.optimization_barrier(jnp.sum(raised, axis=-1, keepdims=True))
        return jnp.einsum('hqk,khd->qhd', low(probs), values_all, precision=lax.Precision.HIGHEST)
    attended = lax.map(jax.checkpoint(attend), (queries.reshape(blocks, block_rows, HEADS, HEAD), seg_row.reshape(blocks, block_rows)))
    attended = attended.reshape(SEQ, HEADS * HEAD) * live_row[:, None]
    attended = low_back(low(attended))
    after_attn = row_in + low_back(product(attended, full_out))
    normed_two = low(rms_norm(after_attn, full_gains[1]))
    gate_val = low_back(product(normed_two, full_gate_up[0]))
    lift = low_back(product(normed_two, full_gate_up[1]))
    hidden = low(jax.nn.gelu(gate_val, approximate=True) * lift)
    return after_attn + low_back(product(hidden, full_down))

def adam_update(weight, moment, second, grad, step_rate, decay):
    moment_new = BETA_ONE * moment + (1.0 - BETA_ONE) * grad
    second_new = BETA_TWO * second + (1.0 - BETA_TWO) * grad * grad
    moment_hat = moment_new / (1.0 - BETA_ONE ** ADAM_STEP)
    second_hat = second_new / (1.0 - BETA_TWO ** ADAM_STEP)
    updated = weight - step_rate * (moment_hat / (jnp.sqrt(second_hat) + ADAM_EPS) + decay * weight)
    return (updated, updated.astype(jnp.bfloat16), moment_new, second_new)

def reference(inputs, cotangent, segment_ids, row_length, w_qkv, m_qkv, v_qkv, w_out, m_out, v_out, w_gate_up, m_gate_up, v_gate_up, w_down, m_down, v_down, norm_gains, m_gains, v_gains):
    masters = (w_qkv, w_out, w_gate_up, w_down, norm_gains)
    weights = tuple((member.astype(jnp.bfloat16).astype(jnp.float32) for member in masters))
    positions = jnp.arange(SEQ, dtype=jnp.int32)

    def one_row(summed, row):
        row_in, row_grad, seg_row, length = row
        live_row = (positions < length).astype(jnp.float32)
        output_row, pullback = jax.vjp(lambda wts, given: row_forward(wts, given, seg_row, live_row), weights, row_in.astype(jnp.float32))
        gradients, input_grad = pullback(row_grad.astype(jnp.float32))
        summed = jax.tree.map(lambda left, right: left + right, summed, gradients)
        return (summed, (output_row, input_grad))
    initial = jax.tree.map(jnp.zeros_like, weights)
    gradients, (block_output, input_grad) = lax.scan(one_row, initial, (inputs, cotangent, segment_ids, row_length))
    moments = (m_qkv, m_out, m_gate_up, m_down, m_gains)
    seconds = (v_qkv, v_out, v_gate_up, v_down, v_gains)
    decays = (DECAY_RATE, DECAY_RATE, DECAY_RATE, DECAY_RATE, 0.0)
    results = [adam_update(masters[index], moments[index], seconds[index], gradients[index], RATES[index], decays[index]) for index in range(5)]
    return (block_output, input_grad, results[0][0], results[0][1], results[0][2], results[0][3], results[1][0], results[1][1], results[1][2], results[1][3], results[2][0], results[2][1], results[2][2], results[2][3], results[3][0], results[3][1], results[3][2], results[3][3], results[4][0], results[4][1], results[4][2], results[4][3])
```

```python
import functools

import jax
import jax.numpy as jnp
from jax import lax
from jax.experimental import pallas as pl
from jax.experimental.pallas import tpu as pltpu
from jax.sharding import PartitionSpec as P

HEAD = 64
ADAM_STEP = 5


EPS_NORM = 1e-06
BETA_ONE = 0.9
BETA_TWO = 0.999
ADAM_EPS = 1e-08
DECAY_RATE = 0.1
RATES = (0.03, 0.5, 0.06, 0.04, 0.4)
NEG_FILL = -1e30


def rms_scale(values_in):
    return lax.rsqrt(jnp.mean(values_in * values_in, axis=-1, keepdims=True) + EPS_NORM)


def norm_back(d_normed, hat, scale, gain):
    scaled = gain * d_normed
    return scale * (scaled - hat * jnp.mean(scaled * hat, axis=-1, keepdims=True))


def gated(gate_val, lift):
    return jax.nn.gelu(gate_val, approximate=True) * lift


def adam_update(weight, moment, second, grad, step_rate, decay):
    moment_new = BETA_ONE * moment + (1.0 - BETA_ONE) * grad
    second_new = BETA_TWO * second + (1.0 - BETA_TWO) * grad * grad
    moment_hat = moment_new / (1.0 - BETA_ONE**ADAM_STEP)
    second_hat = second_new / (1.0 - BETA_TWO**ADAM_STEP)
    updated = weight - step_rate * (moment_hat / (jnp.sqrt(second_hat) + ADAM_EPS) + decay * weight)
    return (updated, updated.astype(jnp.bfloat16), moment_new, second_new)


NT = (((1,), (1,)), ((), ()))
NN = (((1,), (0,)), ((), ()))


def dot32(left, right, dims):
    return lax.dot_general(left, right, dims, preferred_element_type=jnp.float32)


def attend_kernel(lo_ref, hi_ref, q_ref, k_ref, vt_ref, seg_q, seg_k, o_ref, lse_ref, *, bk, heads):
    i = pl.program_id(0)
    bq = q_ref.shape[0]

    def body(j, carry):
        ks = pl.ds(pl.multiple_of(j * bk, bk), bk)
        same = seg_k[ks, :] == seg_q[...]
        out = []
        for h in range(heads):
            peak, total, acc = carry[h]
            hs = slice(h * HEAD, (h + 1) * HEAD)
            s = jnp.where(same, dot32(k_ref[ks, hs], q_ref[:, hs], NT), NEG_FILL)
            peak_new = jnp.maximum(peak, jnp.max(s, axis=0, keepdims=True))
            p = jnp.exp(s - peak_new)
            keep = jnp.exp(peak - peak_new)
            total = total * keep + jnp.sum(p, axis=0, keepdims=True)
            acc = acc * keep + dot32(vt_ref[hs, ks], p.astype(jnp.bfloat16), NN)
            out.append((peak_new, total, acc))
        return tuple(out)

    first = tuple(
        (
            jnp.full((1, bq), NEG_FILL, jnp.float32),
            jnp.zeros((1, bq), jnp.float32),
            jnp.zeros((HEAD, bq), jnp.float32),
        )
        for _ in range(heads)
    )
    found = lax.fori_loop(lo_ref[i], hi_ref[i], body, first)
    totals = [jnp.where(total > 0, total, 1.0) for _, total, _ in found]
    o_ref[...] = jnp.concatenate([acc / t for (_, _, acc), t in zip(found, totals)], axis=0).T
    lse_ref[...] = jnp.concatenate([peak + jnp.log(t) for (peak, _, _), t in zip(found, totals)], axis=0)


def attend(q, k, vt, seg, lo, hi, bq, bk):
    rows, width = q.shape
    heads = width // HEAD
    keys = k.shape[0]
    whole = lambda i, *_: (0, 0)
    return pl.pallas_call(
        functools.partial(attend_kernel, bk=bk, heads=heads),
        out_shape=(
            jax.ShapeDtypeStruct((rows, width), jnp.float32),
            jax.ShapeDtypeStruct((heads, rows), jnp.float32),
        ),
        grid_spec=pltpu.PrefetchScalarGridSpec(
            num_scalar_prefetch=2,
            grid=(rows // bq,),
            in_specs=[
                pl.BlockSpec((bq, width), lambda i, *_: (i, 0)),
                pl.BlockSpec((keys, width), whole),
                pl.BlockSpec((width, keys), whole),
                pl.BlockSpec((1, bq), lambda i, *_: (0, i)),
                pl.BlockSpec((keys, 1), whole),
            ],
            out_specs=(
                pl.BlockSpec((bq, width), lambda i, *_: (i, 0)),
                pl.BlockSpec((heads, bq), lambda i, *_: (0, i)),
            ),
        ),
        name="attend",
    )(lo, hi, q, k, vt, seg[None, :], seg[:, None])


def attend_back_kernel(
    lo_ref, hi_ref, q_ref, do_ref, lse_ref, dot_ref, k_ref, kt_ref, v_ref, seg_q, seg_k,
    dq_ref, dk_ref, dv_ref, dk_sum, dv_sum, *, bk, heads,
):
    i = pl.program_id(0)
    bq = q_ref.shape[0]

    @pl.when(i == 0)
    def _():
        dk_sum[...] = jnp.zeros_like(dk_sum)
        dv_sum[...] = jnp.zeros_like(dv_sum)

    def body(j, carry):
        ks = pl.ds(pl.multiple_of(j * bk, bk), bk)
        same = seg_k[ks, :] == seg_q[...]
        out, dks, dvs = [], [], []
        for h in range(heads):
            hs = slice(h * HEAD, (h + 1) * HEAD)
            qh = q_ref[:, hs]
            doh = do_ref[:, hs]
            s = dot32(k_ref[ks, hs], qh, NT)
            p = jnp.exp(jnp.where(same, s - lse_ref[h : h + 1, :], NEG_FILL))
            dp = dot32(v_ref[ks, hs], doh, NT)
            ds = (p * (dp - dot_ref[h : h + 1, :])).astype(jnp.bfloat16)
            dvs.append(dot32(p.astype(jnp.bfloat16), doh, NN))
            dks.append(dot32(ds, qh, NN))
            out.append(carry[h] + dot32(kt_ref[hs, ks], ds, NN))
        dk_sum[ks, :] += jnp.concatenate(dks, axis=1)
        dv_sum[ks, :] += jnp.concatenate(dvs, axis=1)
        return tuple(out)

    first = tuple(jnp.zeros((HEAD, bq), jnp.float32) for _ in range(heads))
    found = lax.fori_loop(lo_ref[i], hi_ref[i], body, first)
    dq_ref[...] = jnp.concatenate(found, axis=0).T.astype(dq_ref.dtype)

    @pl.when(i == pl.num_programs(0) - 1)
    def _():
        dk_ref[...] = dk_sum[...].astype(dk_ref.dtype)
        dv_ref[...] = dv_sum[...].astype(dv_ref.dtype)


def attend_back(q, k, kt, v, d_out, lse, row_dot, seg, lo, hi, bq, bk):
    rows, width = q.shape
    heads = width // HEAD
    keys = k.shape[0]
    whole = lambda i, *_: (0, 0)
    by_row = lambda i, *_: (i, 0)
    by_col = lambda i, *_: (0, i)
    return pl.pallas_call(
        functools.partial(attend_back_kernel, bk=bk, heads=heads),
        out_shape=(
            jax.ShapeDtypeStruct((rows, width), jnp.bfloat16),
            jax.ShapeDtypeStruct((keys, width), jnp.bfloat16),
            jax.ShapeDtypeStruct((keys, width), jnp.bfloat16),
        ),
        grid_spec=pltpu.PrefetchScalarGridSpec(
            num_scalar_prefetch=2,
            grid=(rows // bq,),
            in_specs=[
                pl.BlockSpec((bq, width), by_row),
                pl.BlockSpec((bq, width), by_row),
                pl.BlockSpec((heads, bq), by_col),
                pl.BlockSpec((heads, bq), by_col),
                pl.BlockSpec((keys, width), whole),
                pl.BlockSpec((width, keys), whole),
                pl.BlockSpec((keys, width), whole),
                pl.BlockSpec((1, bq), by_col),
                pl.BlockSpec((keys, 1), whole),
            ],
            out_specs=(
                pl.BlockSpec((bq, width), by_row),
                pl.BlockSpec((keys, width), whole),
                pl.BlockSpec((keys, width), whole),
            ),
            scratch_shapes=[pltpu.VMEM((keys, width), jnp.float32)] * 2,
        ),
        name="attend_back",
    )(lo, hi, q, d_out, lse, row_dot, k, kt, v, seg[None, :], seg[:, None])


def key_blocks(seg, length, bq, bk):
    lo = jnp.sum(seg[None, :] < seg[::bq][:, None], axis=1)
    hi = jnp.minimum(jnp.sum(seg[None, :] <= seg[bq - 1 :: bq][:, None], axis=1), length)
    lo = lo // bk
    hi = (hi + bk - 1) // bk
    dead = jnp.arange(seg.shape[0] // bq) * bq >= length
    return lo.astype(jnp.int32), jnp.where(dead, lo, hi).astype(jnp.int32)


def on_device(
    inputs,
    cotangent,
    segment_ids,
    row_length,
    w_qkv,
    m_qkv,
    v_qkv,
    w_out,
    m_out,
    v_out,
    w_gate_up,
    m_gate_up,
    v_gate_up,
    w_down,
    m_down,
    v_down,
    norm_gains,
    m_gains,
    v_gains,
):
    copy_qkv = w_qkv.astype(jnp.bfloat16)
    copy_out = w_out.astype(jnp.bfloat16)
    copy_gate_up = w_gate_up.astype(jnp.bfloat16)
    copy_down = w_down.astype(jnp.bfloat16)
    copy_gains = norm_gains.astype(jnp.bfloat16)
    full_qkv, full_out, full_gate_up, full_down, full_gains = (
        lax.all_gather(copy_qkv, "dp", axis=1, tiled=True),
        lax.all_gather(copy_out, "dp", axis=1, tiled=True),
        lax.all_gather(copy_gate_up, "dp", axis=1, tiled=True),
        lax.all_gather(copy_down, "dp", axis=1, tiled=True),
        lax.all_gather(copy_gains, "dp", axis=1, tiled=True),
    )
    gain_one = full_gains[0].astype(jnp.float32)
    gain_two = full_gains[1].astype(jnp.float32)
    seq_len = segment_ids.shape[1]
    width = full_qkv.shape[2]
    heads_here = width // HEAD
    seg_row = segment_ids[0]
    positions = jnp.arange(seq_len, dtype=jnp.int32)
    live_row = (positions < row_length[0]).astype(jnp.float32)
    resid_in = inputs[0].astype(jnp.float32)
    scale_one = rms_scale(resid_in)
    hat_one = resid_in * scale_one
    normed_one = (hat_one * gain_one).astype(jnp.bfloat16)
    qkv_rows = jnp.einsum(
        "td,cdf->tcf",
        lax.all_gather(normed_one, "mp", axis=0, tiled=True),
        full_qkv,
        preferred_element_type=jnp.float32,
    ).astype(jnp.bfloat16)
    queries, keys_all, values_all = qkv_rows[:, 0], qkv_rows[:, 1], qkv_rows[:, 2]
    wide, narrow = min(1024, seq_len), min(512, seq_len)
    lo, hi = key_blocks(seg_row, row_length[0], wide, narrow)
    raw_out, log_sums = attend(queries, keys_all, values_all.T, seg_row, lo, hi, wide, narrow)
    log_sums = jnp.where(live_row[None, :] > 0, log_sums, -NEG_FILL)
    attended = (raw_out * live_row[:, None]).astype(jnp.bfloat16)
    after_attn = resid_in + lax.psum_scatter(
        jnp.dot(attended, full_out, preferred_element_type=jnp.float32).astype(jnp.bfloat16),
        "mp",
        scatter_dimension=0,
        tiled=True,
    ).astype(jnp.float32)
    scale_two = rms_scale(after_attn)
    hat_two = after_attn * scale_two
    normed_two = (hat_two * gain_two).astype(jnp.bfloat16)
    both_rows = jnp.einsum(
        "td,cdf->ctf",
        lax.all_gather(normed_two, "mp", axis=0, tiled=True),
        full_gate_up,
        preferred_element_type=jnp.float32,
    )
    hidden = gated(both_rows[0], both_rows[1]).astype(jnp.bfloat16)
    block_output = after_attn + lax.psum_scatter(
        jnp.dot(hidden, full_down, preferred_element_type=jnp.float32).astype(jnp.bfloat16),
        "mp",
        scatter_dimension=0,
        tiled=True,
    ).astype(jnp.float32)
    grad_all, normed_two_all = (
        lax.all_gather(cotangent[0], "mp", axis=0, tiled=True),
        lax.all_gather(normed_two, "mp", axis=0, tiled=True),
    )
    both_again = jnp.einsum(
        "td,cdf->ctf", normed_two_all, full_gate_up, preferred_element_type=jnp.float32
    )
    hidden_again, gated_pull = jax.vjp(gated, both_again[0], both_again[1])
    hidden_again = hidden_again.astype(jnp.bfloat16)
    d_hidden = jnp.einsum("td,fd->tf", grad_all, full_down, preferred_element_type=jnp.float32)
    d_gate, d_lift = gated_pull(d_hidden)
    d_both = jnp.stack([d_gate, d_lift]).astype(jnp.bfloat16)
    grad_down = jnp.einsum("tf,td->fd", hidden_again, grad_all, preferred_element_type=jnp.float32)
    grad_gate_up = jnp.einsum(
        "td,ctf->cdf", normed_two_all, d_both, preferred_element_type=jnp.float32
    )
    part = d_both
    d_normed_two = lax.psum_scatter(
        jnp.einsum("ctf,cdf->td", part, full_gate_up, preferred_element_type=jnp.float32).astype(
            jnp.bfloat16
        ),
        "mp",
        scatter_dimension=0,
        tiled=True,
    ).astype(jnp.float32)
    d_after = cotangent[0].astype(jnp.float32) + norm_back(
        d_normed_two, hat_two, scale_two, gain_two
    )
    grad_gain_two = jnp.sum(d_normed_two * hat_two, axis=0)
    d_branch = d_after.astype(jnp.bfloat16)
    d_branch_all, normed_one_all = (
        lax.all_gather(d_branch, "mp", axis=0, tiled=True),
        lax.all_gather(normed_one, "mp", axis=0, tiled=True),
    )
    grad_out = jnp.einsum("tf,td->fd", attended, d_branch_all, preferred_element_type=jnp.float32)
    d_attended = jnp.einsum(
        "td,fd->tf", d_branch_all, full_out, preferred_element_type=jnp.float32
    ).astype(jnp.bfloat16)
    d_attended = d_attended * live_row[:, None].astype(jnp.bfloat16)

    row_dot = jnp.sum((raw_out * d_attended).reshape(seq_len, heads_here, HEAD), axis=-1).T
    lo, hi = key_blocks(seg_row, row_length[0], narrow, narrow)
    d_queries, d_keys, d_values = attend_back(
        queries, keys_all, keys_all.T, values_all, d_attended, log_sums, row_dot, seg_row, lo, hi, narrow, narrow
    )
    d_qkv = jnp.stack([d_queries, d_keys, d_values], axis=1)
    grad_qkv = jnp.einsum("td,tcf->cdf", normed_one_all, d_qkv, preferred_element_type=jnp.float32)
    part = d_qkv
    d_normed_one = lax.psum_scatter(
        jnp.einsum("tcf,cdf->td", part, full_qkv, preferred_element_type=jnp.float32).astype(
            jnp.bfloat16
        ),
        "mp",
        scatter_dimension=0,
        tiled=True,
    ).astype(jnp.float32)
    input_grad = d_after + norm_back(d_normed_one, hat_one, scale_one, gain_one)
    grad_gain_one = jnp.sum(d_normed_one * hat_one, axis=0)
    grad_gains = lax.psum(jnp.stack([grad_gain_one, grad_gain_two]), "mp")
    red_qkv, red_out, red_gate_up, red_down, red_gains = (
        lax.psum_scatter(grad_qkv.astype(jnp.bfloat16), "dp", scatter_dimension=1, tiled=True).astype(
            jnp.float32
        ),
        lax.psum_scatter(grad_out.astype(jnp.bfloat16), "dp", scatter_dimension=1, tiled=True).astype(
            jnp.float32
        ),
        lax.psum_scatter(grad_gate_up.astype(jnp.bfloat16), "dp", scatter_dimension=1, tiled=True).astype(
            jnp.float32
        ),
        lax.psum_scatter(grad_down.astype(jnp.bfloat16), "dp", scatter_dimension=1, tiled=True).astype(
            jnp.float32
        ),
        lax.psum_scatter(grad_gains, "dp", scatter_dimension=1, tiled=True),
    )
    new_qkv = adam_update(w_qkv, m_qkv, v_qkv, red_qkv, RATES[0], DECAY_RATE)
    new_out = adam_update(w_out, m_out, v_out, red_out, RATES[1], DECAY_RATE)
    new_gate_up = adam_update(w_gate_up, m_gate_up, v_gate_up, red_gate_up, RATES[2], DECAY_RATE)
    new_down = adam_update(w_down, m_down, v_down, red_down, RATES[3], DECAY_RATE)
    new_gains = adam_update(norm_gains, m_gains, v_gains, red_gains, RATES[4], 0.0)
    return (
        block_output[None],
        input_grad[None],
        new_qkv[0],
        new_qkv[1],
        new_qkv[2],
        new_qkv[3],
        new_out[0],
        new_out[1],
        new_out[2],
        new_out[3],
        new_gate_up[0],
        new_gate_up[1],
        new_gate_up[2],
        new_gate_up[3],
        new_down[0],
        new_down[1],
        new_down[2],
        new_down[3],
        new_gains[0],
        new_gains[1],
        new_gains[2],
        new_gains[3],
    )


def solution(mesh):
    return jax.shard_map(
        on_device,
        mesh=mesh,
        in_specs=(
            P("dp", "mp", None),
            P("dp", "mp", None),
            P("dp", None),
            P("dp"),
            P(None, "dp", "mp"),
            P(None, "dp", "mp"),
            P(None, "dp", "mp"),
            P("mp", "dp"),
            P("mp", "dp"),
            P("mp", "dp"),
            P(None, "dp", "mp"),
            P(None, "dp", "mp"),
            P(None, "dp", "mp"),
            P("mp", "dp"),
            P("mp", "dp"),
            P("mp", "dp"),
            P(None, "dp"),
            P(None, "dp"),
            P(None, "dp"),
        ),
        out_specs=(
            P("dp", "mp", None),
            P("dp", "mp", None),
            P(None, "dp", "mp"),
            P(None, "dp", "mp"),
            P(None, "dp", "mp"),
            P(None, "dp", "mp"),
            P("mp", "dp"),
            P("mp", "dp"),
            P("mp", "dp"),
            P("mp", "dp"),
            P(None, "dp", "mp"),
            P(None, "dp", "mp"),
            P(None, "dp", "mp"),
            P(None, "dp", "mp"),
            P("mp", "dp"),
            P("mp", "dp"),
            P("mp", "dp"),
            P("mp", "dp"),
            P(None, "dp"),
            P(None, "dp"),
            P(None, "dp"),
            P(None, "dp"),
        ),
        check_vma=False,
    )
```

```python
import functools
import math

import jax
import jax.numpy as jnp
from jax import lax
from jax.experimental import pallas as pl
from jax.experimental.pallas import tpu as pltpu
from jax.sharding import PartitionSpec as P

HEAD = 64
ADAM_STEP = 5
LANES = 128


EPS_NORM = 1e-06
BETA_ONE = 0.9
BETA_TWO = 0.999
ADAM_EPS = 1e-08
DECAY_RATE = 0.1
RATES = (0.03, 0.5, 0.06, 0.04, 0.4)
NEG_FILL = -1e30
GELU_IN = 0.7978845608028654
GELU_CUBE = 0.044715


def rms_scale(values_in):
    return lax.rsqrt(jnp.mean(values_in * values_in, axis=-1, keepdims=True) + EPS_NORM)


def norm_back(d_normed, hat, scale, gain):
    scaled = gain * d_normed
    return scale * (scaled - hat * jnp.mean(scaled * hat, axis=-1, keepdims=True))


def adam_update(weight, moment, second, grad, step_rate, decay):
    moment_new = BETA_ONE * moment + (1.0 - BETA_ONE) * grad
    second_new = BETA_TWO * second + (1.0 - BETA_TWO) * grad * grad
    moment_hat = moment_new / (1.0 - BETA_ONE**ADAM_STEP)
    second_hat = second_new / (1.0 - BETA_TWO**ADAM_STEP)
    updated = weight - step_rate * (moment_hat / (jnp.sqrt(second_hat) + ADAM_EPS) + decay * weight)
    return (updated, updated.astype(jnp.bfloat16), moment_new, second_new)


NT = (((1,), (1,)), ((), ()))
NN = (((1,), (0,)), ((), ()))


def dot32(left, right, dims):
    return lax.dot_general(left, right, dims, preferred_element_type=jnp.float32)


def attend_kernel(lo_ref, hi_ref, q_ref, k_ref, v_ref, seg_q, seg_k, o_ref, lse_ref, vt_ref, *, bk, heads):
    i = pl.program_id(0)
    bq = q_ref.shape[0]

    @pl.when(i == 0)
    def _():
        vt_ref[...] = v_ref[...].T

    def body(j, carry):
        ks = pl.ds(pl.multiple_of(j * bk, bk), bk)
        same = seg_k[ks, :] == seg_q[...]
        out = []
        for h in range(heads):
            peak, total, acc = carry[h]
            hs = slice(h * HEAD, (h + 1) * HEAD)
            s = jnp.where(same, dot32(k_ref[ks, hs], q_ref[:, hs], NT), NEG_FILL)
            peak_new = jnp.maximum(peak, jnp.max(s, axis=0, keepdims=True))
            p = jnp.exp(s - peak_new)
            keep = jnp.exp(peak - peak_new)
            total = total * keep + jnp.sum(p, axis=0, keepdims=True)
            acc = acc * keep + dot32(vt_ref[hs, ks], p.astype(jnp.bfloat16), NN)
            out.append((peak_new, total, acc))
        return tuple(out)

    first = tuple(
        (
            jnp.full((1, bq), NEG_FILL, jnp.float32),
            jnp.zeros((1, bq), jnp.float32),
            jnp.zeros((HEAD, bq), jnp.float32),
        )
        for _ in range(heads)
    )
    found = lax.fori_loop(lo_ref[i], hi_ref[i], body, first)
    totals = [jnp.where(total > 0, total, 1.0) for _, total, _ in found]
    o_ref[...] = jnp.concatenate([acc / t for (_, _, acc), t in zip(found, totals)], axis=0).T
    lse_ref[...] = jnp.concatenate([peak + jnp.log(t) for (peak, _, _), t in zip(found, totals)], axis=0)


def attend(qkv, seg, lo, hi, bq, bk):
    rows, width = qkv.shape[0], qkv.shape[1] // 3
    heads = width // HEAD
    return pl.pallas_call(
        functools.partial(attend_kernel, bk=bk, heads=heads),
        out_shape=(
            jax.ShapeDtypeStruct((rows, width), jnp.float32),
            jax.ShapeDtypeStruct((heads, rows), jnp.float32),
        ),
        grid_spec=pltpu.PrefetchScalarGridSpec(
            num_scalar_prefetch=2,
            grid=(rows // bq,),
            in_specs=[
                pl.BlockSpec((bq, width), lambda i, *_: (i, 0)),
                pl.BlockSpec((rows, width), lambda i, *_: (0, 1)),
                pl.BlockSpec((rows, width), lambda i, *_: (0, 2)),
                pl.BlockSpec((1, bq), lambda i, *_: (0, i)),
                pl.BlockSpec((rows, 1), lambda i, *_: (0, 0)),
            ],
            out_specs=(
                pl.BlockSpec((bq, width), lambda i, *_: (i, 0)),
                pl.BlockSpec((heads, bq), lambda i, *_: (0, i)),
            ),
            scratch_shapes=[pltpu.VMEM((width, rows), jnp.bfloat16)],
        ),
        name="attend",
    )(lo, hi, qkv, qkv, qkv, seg[None, :], seg[:, None])


def attend_back_kernel(
    lo_ref, hi_ref, q_ref, do_ref, lse_ref, dot_ref, k_ref, v_ref, seg_q, seg_k,
    d_ref, dk_sum, dv_sum, kt_ref, *, bk, heads,
):
    i = pl.program_id(0)
    bq, width = q_ref.shape

    @pl.when(i == 0)
    def _():
        kt_ref[...] = k_ref[...].T
        dk_sum[...] = jnp.zeros_like(dk_sum)
        dv_sum[...] = jnp.zeros_like(dv_sum)

    def body(j, carry):
        ks = pl.ds(pl.multiple_of(j * bk, bk), bk)
        same = seg_k[ks, :] == seg_q[...]
        out, dks, dvs = [], [], []
        for h in range(heads):
            hs = slice(h * HEAD, (h + 1) * HEAD)
            qh = q_ref[:, hs]
            doh = do_ref[:, hs]
            s = dot32(k_ref[ks, hs], qh, NT)
            p = jnp.exp(jnp.where(same, s - lse_ref[h : h + 1, :], NEG_FILL))
            dp = dot32(v_ref[ks, hs], doh, NT)
            ds = (p * (dp - dot_ref[h : h + 1, :])).astype(jnp.bfloat16)
            dvs.append(dot32(p.astype(jnp.bfloat16), doh, NN))
            dks.append(dot32(ds, qh, NN))
            out.append(carry[h] + dot32(kt_ref[hs, ks], ds, NN))
        dk_sum[ks, :] += jnp.concatenate(dks, axis=1)
        dv_sum[ks, :] += jnp.concatenate(dvs, axis=1)
        return tuple(out)

    first = tuple(jnp.zeros((HEAD, bq), jnp.float32) for _ in range(heads))
    found = lax.fori_loop(lo_ref[i], hi_ref[i], body, first)
    d_ref[pl.ds(pl.multiple_of(i * bq, bq), bq), :width] = jnp.concatenate(found, axis=0).T.astype(d_ref.dtype)

    @pl.when(i == pl.num_programs(0) - 1)
    def _():
        d_ref[:, width : 2 * width] = dk_sum[...].astype(d_ref.dtype)
        d_ref[:, 2 * width :] = dv_sum[...].astype(d_ref.dtype)


def attend_back(qkv, d_out, lse, row_dot, seg, lo, hi, bq, bk):
    rows, width = d_out.shape
    heads = width // HEAD
    by_row = lambda i, *_: (i, 0)
    by_col = lambda i, *_: (0, i)
    return pl.pallas_call(
        functools.partial(attend_back_kernel, bk=bk, heads=heads),
        out_shape=jax.ShapeDtypeStruct((rows, 3 * width), jnp.bfloat16),
        grid_spec=pltpu.PrefetchScalarGridSpec(
            num_scalar_prefetch=2,
            grid=(rows // bq,),
            in_specs=[
                pl.BlockSpec((bq, width), by_row),
                pl.BlockSpec((bq, width), by_row),
                pl.BlockSpec((heads, bq), by_col),
                pl.BlockSpec((heads, bq), by_col),
                pl.BlockSpec((rows, width), lambda i, *_: (0, 1)),
                pl.BlockSpec((rows, width), lambda i, *_: (0, 2)),
                pl.BlockSpec((1, bq), by_col),
                pl.BlockSpec((rows, 1), lambda i, *_: (0, 0)),
            ],
            out_specs=pl.BlockSpec((rows, 3 * width), lambda i, *_: (0, 0)),
            scratch_shapes=[
                pltpu.VMEM((rows, width), jnp.float32),
                pltpu.VMEM((rows, width), jnp.float32),
                pltpu.VMEM((width, rows), jnp.bfloat16),
            ],
        ),
        name="attend_back",
    )(lo, hi, qkv, d_out, lse, row_dot, qkv, qkv, seg[None, :], seg[:, None])


def key_blocks(seg, length, bq, bk):
    lo = jnp.sum(seg[None, :] < seg[::bq][:, None], axis=1)
    hi = jnp.minimum(jnp.sum(seg[None, :] <= seg[bq - 1 :: bq][:, None], axis=1), length)
    lo = lo // bk
    hi = (hi + bk - 1) // bk
    dead = jnp.arange(seg.shape[0] // bq) * bq >= length
    return lo.astype(jnp.int32), jnp.where(dead, lo, hi).astype(jnp.int32)


TN = (((0,), (0,)), ((), ()))
PIECES = 8


def feed_kernel(spots, *refs, slices):
    n_ref, g_ref = refs[:2]
    w_in = [refs[2 + 4 * s : 6 + 4 * s] for s in range(slices)]
    at = 2 + 4 * slices
    out_ref, dn_ref = refs[at : at + 2]
    d_out = [refs[at + 2 + 4 * s : at + 6 + 4 * s] for s in range(slices)]
    w_buf, d_buf, w_sem, d_sem = refs[at + 2 + 4 * slices :]
    step = pl.program_id(0)
    slot = lax.rem(step, 2)

    def pieces(arrays, s, buf, sem, outward):
        held = s % 2
        for p in range(PIECES):
            lanes = pl.ds(pl.multiple_of(spots[s * PIECES + p] * LANES, LANES), LANES)
            far = arrays[p // 2].at[p % 2]
            near = buf.at[held, :, :, lanes]
            src, dst = (near, far) if outward else (far, near)
            yield pltpu.make_async_copy(src, dst, sem.at[held])

    for s in range(slices):

        @pl.when(step == s)
        def _(s=s):
            if s == 0:
                for first in range(min(2, slices)):
                    for copy in pieces(w_in[first], first, w_buf, w_sem, False):
                        copy.start()
            for copy in pieces(w_in[s], s, w_buf, w_sem, False):
                copy.wait()

    @pl.when(step == 0)
    def _():
        out_ref[...] = jnp.zeros_like(out_ref)
        dn_ref[...] = jnp.zeros_like(dn_ref)

    n = n_ref[...]
    g = g_ref[...]
    gate = dot32(n, w_buf[slot, 0], NT)
    up = dot32(n, w_buf[slot, 1], NT)
    d_hidden = dot32(g, w_buf[slot, 2], NT)
    square = gate * gate
    bent = jnp.tanh(gate * (GELU_IN + (GELU_IN * GELU_CUBE) * square))
    half = 0.5 + 0.5 * bent
    lifted = gate * half
    slope = half + (0.5 * gate) * (1.0 - bent * bent) * (GELU_IN + (3.0 * GELU_IN * GELU_CUBE) * square)
    hidden = (lifted * up).astype(jnp.bfloat16)
    d_gate = (d_hidden * up * slope).astype(jnp.bfloat16)
    d_up = (d_hidden * lifted).astype(jnp.bfloat16)
    out_ref[...] += dot32(hidden, w_buf[slot, 2], NN)
    dn_ref[...] += dot32(d_gate, w_buf[slot, 0], NN) + dot32(d_up, w_buf[slot, 1], NN)

    for s in range(2, slices):

        @pl.when(step == s)
        def _(s=s):
            for copy in pieces(d_out[s - 2], s - 2, d_buf, d_sem, True):
                copy.wait()

    d_buf[slot, 2] = dot32(hidden, g, TN).astype(jnp.bfloat16)
    d_buf[slot, 0] = dot32(d_gate, n, TN).astype(jnp.bfloat16)
    d_buf[slot, 1] = dot32(d_up, n, TN).astype(jnp.bfloat16)

    for s in range(slices):

        @pl.when(step == s)
        def _(s=s):
            for copy in pieces(d_out[s], s, d_buf, d_sem, True):
                copy.start()
            if s + 2 < slices:
                for copy in pieces(w_in[s + 2], s + 2, w_buf, w_sem, False):
                    copy.start()
            if s == slices - 1:
                for last in range(max(0, slices - 2), slices):
                    for copy in pieces(d_out[last], last, d_buf, d_sem, True):
                        copy.wait()


def feed(n, g, weights, spots):
    slices = len(weights)
    rows, width = n.shape
    hidden = weights[0][0].shape[2]
    whole = pl.BlockSpec((rows, width), lambda i, *_: (0, 0))
    there = pl.BlockSpec(memory_space=pl.ANY)
    acc = jax.ShapeDtypeStruct((rows, width), jnp.float32)
    part = jax.ShapeDtypeStruct((2, 3, hidden, LANES), jnp.bfloat16)
    found = pl.pallas_call(
        functools.partial(feed_kernel, slices=slices),
        out_shape=(acc, acc) + (part,) * (4 * slices),
        grid_spec=pltpu.PrefetchScalarGridSpec(
            num_scalar_prefetch=1,
            grid=(slices,),
            in_specs=[whole, whole] + [there] * (4 * slices),
            out_specs=(whole, whole) + (there,) * (4 * slices),
            scratch_shapes=[
                pltpu.VMEM((2, 3, hidden, width), jnp.bfloat16),
                pltpu.VMEM((2, 3, hidden, width), jnp.bfloat16),
                pltpu.SemaphoreType.DMA((2,)),
                pltpu.SemaphoreType.DMA((2,)),
            ],
        ),
        name="feed",
    )(spots, n, g, *[array for slice_ in weights for array in slice_])
    return found[0], found[1], [found[2 + 4 * s : 6 + 4 * s] for s in range(slices)]


def swap_over(axis, count, bit):
    return [(i, i ^ bit) for i in range(count)]


def spots_of(me, chip_bits):
    rows = []
    for first, second in chip_bits:
        rows += [0, first, second, first | second, 1, 1 | first, 1 | second, 1 | first | second]
    return jnp.bitwise_xor(me, jnp.array(rows, jnp.int32))


def gather_slice(piece, count, first, second):
    swap = lambda value, bit: lax.ppermute(value, "dp", swap_over("dp", count, bit))
    pair = jnp.stack([piece, swap(piece, first)])
    other = swap(pair, second)
    return [pair, other, swap(pair, 1), swap(other, 1)]


def scatter_slice(parts, count, first, second):
    swap = lambda value, bit: lax.ppermute(value, "dp", swap_over("dp", count, bit))
    low = lambda value: value.astype(jnp.bfloat16)
    wide = lambda value: value.astype(jnp.float32)
    away = low(wide(parts[1]) + wide(swap(parts[3], 1)))
    near = wide(parts[0]) + wide(swap(parts[2], 1))
    near = near + wide(swap(away, second))
    return near[0] + wide(swap(low(near[1]), first))


def on_device(
    inputs, cotangent, segment_ids, row_length,
    w_qkv, m_qkv, v_qkv, w_out, m_out, v_out, w_gate_up, m_gate_up, v_gate_up, w_down, m_down, v_down,
    norm_gains, m_gains, v_gains,
    *, dp, mp,
):
    f32, bf16 = jnp.float32, jnp.bfloat16
    z = lax.axis_index("mp")
    me = lax.axis_index("dp")
    onward = [(i, (i + 1) % mp) for i in range(mp)]
    ring = lambda value: lax.ppermute(value, "mp", onward)
    rows, width = inputs.shape[1:]
    seq_len = segment_ids.shape[1]
    hidden_here = w_down.shape[0]
    lanes_here = w_down.shape[1]
    heads_width = w_out.shape[0]
    exchange = dp == PIECES and lanes_here == LANES

    copy_qkv = w_qkv.astype(bf16).transpose(0, 2, 1).reshape(3 * heads_width, lanes_here)
    copy_out = w_out.astype(bf16)
    copy_feed = jnp.concatenate([w_gate_up.astype(bf16).transpose(0, 2, 1), w_down.astype(bf16)[None]])
    copy_gains = jnp.pad(norm_gains.astype(bf16), ((0, 14), (0, 0)))

    blocks = [inputs[0]]
    for _ in range(mp - 1):
        blocks.append(ring(blocks[-1]))

    full_first = lax.all_gather(jnp.concatenate([copy_qkv, copy_gains]), "dp", axis=1, tiled=True)
    full_qkv = full_first[: 3 * heads_width]
    gain_one = full_first[3 * heads_width].astype(f32)
    gain_two = full_first[3 * heads_width + 1].astype(f32)
    full_out = lax.all_gather(copy_out, ("dp", "mp"), axis=0)
    full_out = full_out.reshape(dp, mp, heads_width, lanes_here).transpose(1, 2, 0, 3).reshape(mp * heads_width, width)

    copy_feed, _ = lax.optimization_barrier((copy_feed, blocks[-1]))
    feed_own = [copy_feed]
    for _ in range(mp - 1):
        feed_own.append(ring(feed_own[-1]))
    if exchange:
        chip_bits = [(2, 4) if s % 2 == 0 else (4, 2) for s in range(mp)]
        feed_full = [gather_slice(piece, dp, *bits) for piece, bits in zip(feed_own, chip_bits)]
        spots = spots_of(me, chip_bits)
    else:
        chip_bits = [(2, 4)] * mp
        spots = spots_of(0, chip_bits)
        turn = jnp.array([0, 2, 4, 6, 1, 3, 5, 7])
        feed_full = []
        for piece in feed_own:
            whole = lax.all_gather(piece, "dp", axis=2, tiled=True)
            whole = whole.reshape(3, hidden_here, PIECES, LANES).transpose(2, 0, 1, 3)[turn]
            feed_full.append([whole[2 * i : 2 * i + 2] for i in range(4)])

    seg_row = segment_ids[0]
    live_row = jnp.arange(seq_len, dtype=jnp.int32) < row_length[0]
    live = live_row.astype(f32)[:, None]

    resid_in = inputs[0].astype(f32)
    scale_one = rms_scale(resid_in)
    hat_one = resid_in * scale_one
    hats = []
    normed_one = jnp.zeros((seq_len, width), bf16)
    for s, block in enumerate(blocks):
        block = block.astype(f32)
        hats.append(block * rms_scale(block))
        at = lax.rem(z + mp - s, mp) * rows
        normed_one = lax.dynamic_update_slice(normed_one, (hats[-1] * gain_one).astype(bf16), (at, 0))
    qkv = dot32(normed_one, full_qkv, NT).astype(bf16)

    wide, narrow = min(1024, seq_len), min(512, seq_len)
    lo, hi = key_blocks(seg_row, row_length[0], wide, narrow)
    raw_out, log_sums = attend(qkv, seg_row, lo, hi, wide, narrow)
    log_sums = jnp.where(live_row[None, :], log_sums, -NEG_FILL)
    attended = (raw_out * live).astype(bf16)
    attended = lax.all_to_all(attended, "mp", split_axis=0, concat_axis=1, tiled=True)

    after_attn = resid_in + dot32(attended, full_out, NN)
    scale_two = rms_scale(after_attn)
    hat_two = after_attn * scale_two
    normed_two = (hat_two * gain_two).astype(bf16)

    fed, d_normed_two, d_feed = [], [], []
    for start in range(0, mp, 2):
        stop = min(start + 2, mp)
        out_part, d_part, grads = feed(
            normed_two, cotangent[0], feed_full[start:stop], spots[PIECES * start : PIECES * stop]
        )
        fed.append(out_part)
        d_normed_two.append(d_part)
        d_feed += grads
    block_output = after_attn + functools.reduce(jnp.add, fed)
    d_normed_two = functools.reduce(jnp.add, d_normed_two)
    d_after = cotangent[0].astype(f32) + norm_back(d_normed_two, hat_two, scale_two, gain_two)
    grad_gain_two = jnp.sum(d_normed_two * hat_two, axis=0)

    d_branch = d_after.astype(bf16)
    d_attended = dot32(d_branch, full_out, NT).astype(bf16)
    d_attended = lax.all_to_all(d_attended, "mp", split_axis=1, concat_axis=0, tiled=True)
    d_attended = jnp.where(live_row[:, None], d_attended, jnp.zeros((), bf16))
    grad_out = dot32(attended, d_branch, TN).astype(bf16)
    grad_out = lax.psum_scatter(grad_out, "dp", scatter_dimension=1, tiled=True)
    grad_out = lax.psum_scatter(grad_out, "mp", scatter_dimension=0, tiled=True).astype(f32)

    row_dot = jnp.sum((raw_out * d_attended).reshape(seq_len, heads_width // HEAD, HEAD), axis=-1).T
    lo, hi = key_blocks(seg_row, row_length[0], narrow, narrow)
    d_qkv = attend_back(qkv, d_attended, log_sums, row_dot, seg_row, lo, hi, narrow, narrow)

    total = None
    grad_gain_one = jnp.zeros((width,), f32)
    for s in [*range(1, mp), 0]:
        at = lax.rem(z + mp - s, mp) * rows
        part = dot32(lax.dynamic_slice(d_qkv, (at, 0), (rows, d_qkv.shape[1])), full_qkv, NN)
        grad_gain_one = grad_gain_one + jnp.sum(part * hats[s], axis=0)
        total = part if total is None else ring(total.astype(bf16)).astype(f32) + part
    d_normed_one = total
    input_grad = d_after + norm_back(d_normed_one, hat_one, scale_one, gain_one)

    grad_qkv = dot32(d_qkv, normed_one, TN).astype(bf16)
    grad_qkv = lax.psum_scatter(grad_qkv, "dp", scatter_dimension=1, tiled=True).astype(f32)
    grad_qkv = grad_qkv.reshape(3, heads_width, lanes_here).transpose(0, 2, 1)

    if exchange:
        owned = [scatter_slice(parts, dp, *bits) for parts, bits in zip(d_feed, chip_bits)]
    else:
        back = jnp.array([0, 4, 1, 5, 2, 6, 3, 7])
        owned = []
        for parts in d_feed:
            whole = jnp.concatenate(parts)[back].transpose(1, 2, 0, 3).reshape(3, hidden_here, width)
            owned.append(lax.psum_scatter(whole, "dp", scatter_dimension=2, tiled=True).astype(f32))
    total = owned[1]
    for s in [*range(2, mp), 0]:
        total = ring(total.astype(bf16)).astype(f32) + owned[s]
    grad_gate_up = total[:2].transpose(0, 2, 1)
    grad_down = total[2]

    grad_gains = jnp.stack([grad_gain_one, grad_gain_two])
    for axis, count in (("mp", mp), ("dp", dp)):
        bit = 1
        while bit < count:
            grad_gains = grad_gains + lax.ppermute(grad_gains, axis, swap_over(axis, count, bit))
            bit *= 2
    grad_gains = lax.dynamic_slice(grad_gains, (0, me * lanes_here), (2, lanes_here))

    new_qkv = adam_update(w_qkv, m_qkv, v_qkv, grad_qkv, RATES[0], DECAY_RATE)
    new_out = adam_update(w_out, m_out, v_out, grad_out, RATES[1], DECAY_RATE)
    new_gate_up = adam_update(w_gate_up, m_gate_up, v_gate_up, grad_gate_up, RATES[2], DECAY_RATE)
    new_down = adam_update(w_down, m_down, v_down, grad_down, RATES[3], DECAY_RATE)
    new_gains = adam_update(norm_gains, m_gains, v_gains, grad_gains, RATES[4], 0.0)
    return (block_output[None], input_grad[None], *new_qkv, *new_out, *new_gate_up, *new_down, *new_gains)


def solution(mesh):
    tokens = P("dp", "mp", None)
    stacked = P(None, "dp", "mp")
    flat = P("mp", "dp")
    gains = P(None, "dp")
    return jax.shard_map(
        functools.partial(on_device, dp=mesh.shape["dp"], mp=mesh.shape["mp"]),
        mesh=mesh,
        in_specs=(tokens, tokens, P("dp", None), P("dp"))
        + (stacked,) * 3 + (flat,) * 3 + (stacked,) * 3 + (flat,) * 3 + (gains,) * 3,
        out_specs=(tokens, tokens) + (stacked,) * 4 + (flat,) * 4 + (stacked,) * 4 + (flat,) * 4 + (gains,) * 4,
        check_vma=False,
    )
```

```python
import functools
import math

import jax
import jax.numpy as jnp
from jax import lax
from jax.experimental import pallas as pl
from jax.experimental.pallas import tpu as pltpu
from jax.sharding import PartitionSpec as P

HEAD = 64
ADAM_STEP = 5
LANES = 128


EPS_NORM = 1e-06
BETA_ONE = 0.9
BETA_TWO = 0.999
ADAM_EPS = 1e-08
DECAY_RATE = 0.1
RATES = (0.03, 0.5, 0.06, 0.04, 0.4)
NEG_FILL = -1e30
GELU_IN = 0.7978845608028654
GELU_CUBE = 0.044715


def rms_scale(values_in):
    return lax.rsqrt(jnp.mean(values_in * values_in, axis=-1, keepdims=True) + EPS_NORM)


def norm_back(d_normed, hat, scale, gain):
    scaled = gain * d_normed
    return scale * (scaled - hat * jnp.mean(scaled * hat, axis=-1, keepdims=True))


def adam_update(weight, moment, second, grad, step_rate, decay):
    moment_new = BETA_ONE * moment + (1.0 - BETA_ONE) * grad
    second_new = BETA_TWO * second + (1.0 - BETA_TWO) * grad * grad
    moment_hat = moment_new / (1.0 - BETA_ONE**ADAM_STEP)
    second_hat = second_new / (1.0 - BETA_TWO**ADAM_STEP)
    updated = weight - step_rate * (moment_hat / (jnp.sqrt(second_hat) + ADAM_EPS) + decay * weight)
    return (updated, updated.astype(jnp.bfloat16), moment_new, second_new)


NT = (((1,), (1,)), ((), ()))
NN = (((1,), (0,)), ((), ()))


def dot32(left, right, dims):
    return lax.dot_general(left, right, dims, preferred_element_type=jnp.float32)


def attend_kernel(lo_ref, hi_ref, q_ref, k_ref, v_ref, seg_q, seg_k, o_ref, lse_ref, vt_ref, *, bk, heads):
    i = pl.program_id(0)
    bq = q_ref.shape[0]

    @pl.when(i == 0)
    def _():
        vt_ref[...] = v_ref[...].T

    def body(j, carry):
        ks = pl.ds(pl.multiple_of(j * bk, bk), bk)
        same = seg_k[ks, :] == seg_q[...]
        out = []
        for h in range(heads):
            peak, total, acc = carry[h]
            hs = slice(h * HEAD, (h + 1) * HEAD)
            s = jnp.where(same, dot32(k_ref[ks, hs], q_ref[:, hs], NT), NEG_FILL)
            peak_new = jnp.maximum(peak, jnp.max(s, axis=0, keepdims=True))
            p = jnp.exp(s - peak_new)
            keep = jnp.exp(peak - peak_new)
            total = total * keep + jnp.sum(p, axis=0, keepdims=True)
            acc = acc * keep + dot32(vt_ref[hs, ks], p.astype(jnp.bfloat16), NN)
            out.append((peak_new, total, acc))
        return tuple(out)

    first = tuple(
        (
            jnp.full((1, bq), NEG_FILL, jnp.float32),
            jnp.zeros((1, bq), jnp.float32),
            jnp.zeros((HEAD, bq), jnp.float32),
        )
        for _ in range(heads)
    )
    found = lax.fori_loop(lo_ref[i], hi_ref[i], body, first)
    totals = [jnp.where(total > 0, total, 1.0) for _, total, _ in found]
    o_ref[...] = jnp.concatenate([acc / t for (_, _, acc), t in zip(found, totals)], axis=0).T
    lse_ref[...] = jnp.concatenate([peak + jnp.log(t) for (peak, _, _), t in zip(found, totals)], axis=0)


def attend(qkv, group, width, seg, lo, hi, bq, bk):
    rows = qkv.shape[0]
    heads = width // HEAD
    return pl.pallas_call(
        functools.partial(attend_kernel, bk=bk, heads=heads),
        out_shape=(
            jax.ShapeDtypeStruct((rows, width), jnp.float32),
            jax.ShapeDtypeStruct((heads, rows), jnp.float32),
        ),
        grid_spec=pltpu.PrefetchScalarGridSpec(
            num_scalar_prefetch=2,
            grid=(rows // bq,),
            in_specs=[
                pl.BlockSpec((bq, width), lambda i, *_: (i, 3 * group)),
                pl.BlockSpec((rows, width), lambda i, *_: (0, 3 * group + 1)),
                pl.BlockSpec((rows, width), lambda i, *_: (0, 3 * group + 2)),
                pl.BlockSpec((1, bq), lambda i, *_: (0, i)),
                pl.BlockSpec((rows, 1), lambda i, *_: (0, 0)),
            ],
            out_specs=(
                pl.BlockSpec((bq, width), lambda i, *_: (i, 0)),
                pl.BlockSpec((heads, bq), lambda i, *_: (0, i)),
            ),
            scratch_shapes=[pltpu.VMEM((width, rows), jnp.bfloat16)],
        ),
        cost_estimate=pl.CostEstimate(
            flops=16 * heads * rows * rows * HEAD, transcendentals=heads * rows * rows, bytes_accessed=10 * rows * width
        ),
        name="attend",
    )(lo, hi, qkv, qkv, qkv, seg[None, :], seg[:, None])


def attend_back_kernel(
    lo_ref, hi_ref, q_ref, do_ref, lse_ref, dot_ref, k_ref, v_ref, seg_q, seg_k,
    d_ref, dk_sum, dv_sum, kt_ref, *, bk, heads,
):
    i = pl.program_id(0)
    bq, width = q_ref.shape

    @pl.when(i == 0)
    def _():
        kt_ref[...] = k_ref[...].T
        dk_sum[...] = jnp.zeros_like(dk_sum)
        dv_sum[...] = jnp.zeros_like(dv_sum)

    def body(j, carry):
        ks = pl.ds(pl.multiple_of(j * bk, bk), bk)
        same = seg_k[ks, :] == seg_q[...]
        out, dks, dvs = [], [], []
        for h in range(heads):
            hs = slice(h * HEAD, (h + 1) * HEAD)
            qh = q_ref[:, hs]
            doh = do_ref[:, hs]
            s = dot32(k_ref[ks, hs], qh, NT)
            p = jnp.exp(jnp.where(same, s - lse_ref[h : h + 1, :], NEG_FILL))
            dp = dot32(v_ref[ks, hs], doh, NT)
            ds = (p * (dp - dot_ref[h : h + 1, :])).astype(jnp.bfloat16)
            dvs.append(dot32(p.astype(jnp.bfloat16), doh, NN))
            dks.append(dot32(ds, qh, NN))
            out.append(carry[h] + dot32(kt_ref[hs, ks], ds, NN))
        dk_sum[ks, :] += jnp.concatenate(dks, axis=1)
        dv_sum[ks, :] += jnp.concatenate(dvs, axis=1)
        return tuple(out)

    first = tuple(jnp.zeros((HEAD, bq), jnp.float32) for _ in range(heads))
    found = lax.fori_loop(lo_ref[i], hi_ref[i], body, first)
    d_ref[pl.ds(pl.multiple_of(i * bq, bq), bq), :width] = jnp.concatenate(found, axis=0).T.astype(d_ref.dtype)

    @pl.when(i == pl.num_programs(0) - 1)
    def _():
        d_ref[:, width : 2 * width] = dk_sum[...].astype(d_ref.dtype)
        d_ref[:, 2 * width :] = dv_sum[...].astype(d_ref.dtype)


def attend_back(qkv, group, d_out, lse, row_dot, seg, lo, hi, bq, bk):
    rows, width = d_out.shape
    heads = width // HEAD
    by_row = lambda i, *_: (i, 0)
    by_col = lambda i, *_: (0, i)
    return pl.pallas_call(
        functools.partial(attend_back_kernel, bk=bk, heads=heads),
        out_shape=jax.ShapeDtypeStruct((rows, 3 * width), jnp.bfloat16),
        grid_spec=pltpu.PrefetchScalarGridSpec(
            num_scalar_prefetch=2,
            grid=(rows // bq,),
            in_specs=[
                pl.BlockSpec((bq, width), lambda i, *_: (i, 3 * group)),
                pl.BlockSpec((bq, width), by_row),
                pl.BlockSpec((heads, bq), by_col),
                pl.BlockSpec((heads, bq), by_col),
                pl.BlockSpec((rows, width), lambda i, *_: (0, 3 * group + 1)),
                pl.BlockSpec((rows, width), lambda i, *_: (0, 3 * group + 2)),
                pl.BlockSpec((1, bq), by_col),
                pl.BlockSpec((rows, 1), lambda i, *_: (0, 0)),
            ],
            out_specs=pl.BlockSpec((rows, 3 * width), lambda i, *_: (0, 0)),
            scratch_shapes=[
                pltpu.VMEM((rows, width), jnp.float32),
                pltpu.VMEM((rows, width), jnp.float32),
                pltpu.VMEM((width, rows), jnp.bfloat16),
            ],
        ),
        cost_estimate=pl.CostEstimate(
            flops=40 * heads * rows * rows * HEAD, transcendentals=heads * rows * rows, bytes_accessed=16 * rows * width
        ),
        name="attend_back",
    )(lo, hi, qkv, d_out, lse, row_dot, qkv, qkv, seg[None, :], seg[:, None])


def key_blocks(seg, length, bq, bk):
    lo = jnp.sum(seg[None, :] < seg[::bq][:, None], axis=1)
    hi = jnp.minimum(jnp.sum(seg[None, :] <= seg[bq - 1 :: bq][:, None], axis=1), length)
    lo = lo // bk
    hi = (hi + bk - 1) // bk
    dead = jnp.arange(seg.shape[0] // bq) * bq >= length
    return lo.astype(jnp.int32), jnp.where(dead, lo, hi).astype(jnp.int32)


TN = (((0,), (0,)), ((), ()))
PIECES = 8


def feed_kernel(spots, *refs, slices):
    n_ref, g_ref = refs[:2]
    w_in = [refs[2 + PIECES * s : 2 + PIECES * (s + 1)] for s in range(slices)]
    at = 2 + PIECES * slices
    out_ref, dn_ref = refs[at : at + 2]
    d_out = [refs[at + 2 + 4 * s : at + 6 + 4 * s] for s in range(slices)]
    w_buf, d_buf, w_sem, d_sem = refs[at + 2 + 4 * slices :]
    step = pl.program_id(0)
    slot = lax.rem(step, 2)

    def pieces(arrays, s, buf, sem, outward):
        held = s % 2
        for p in range(PIECES):
            lanes = pl.ds(pl.multiple_of(spots[s * PIECES + p] * LANES, LANES), LANES)
            near = buf.at[held, :, :, lanes]
            src, dst = (near, arrays[p // 2].at[p % 2]) if outward else (arrays[p], near)
            yield pltpu.make_async_copy(src, dst, sem.at[held])

    for s in range(slices):

        @pl.when(step == s)
        def _(s=s):
            if s == 0:
                for first in range(min(2, slices)):
                    for copy in pieces(w_in[first], first, w_buf, w_sem, False):
                        copy.start()
            for copy in pieces(w_in[s], s, w_buf, w_sem, False):
                copy.wait()

    @pl.when(step == 0)
    def _():
        out_ref[...] = jnp.zeros_like(out_ref)
        dn_ref[...] = jnp.zeros_like(dn_ref)

    n = n_ref[...]
    g = g_ref[...]
    gate = dot32(n, w_buf[slot, 0], NT)
    up = dot32(n, w_buf[slot, 1], NT)
    d_hidden = dot32(g, w_buf[slot, 2], NT)
    square = gate * gate
    bent = jnp.tanh(gate * (GELU_IN + (GELU_IN * GELU_CUBE) * square))
    half = 0.5 + 0.5 * bent
    lifted = gate * half
    slope = half + (0.5 * gate) * (1.0 - bent * bent) * (GELU_IN + (3.0 * GELU_IN * GELU_CUBE) * square)
    hidden = (lifted * up).astype(jnp.bfloat16)
    d_gate = (d_hidden * up * slope).astype(jnp.bfloat16)
    d_up = (d_hidden * lifted).astype(jnp.bfloat16)
    out_ref[...] += dot32(hidden, w_buf[slot, 2], NN)
    dn_ref[...] += dot32(d_gate, w_buf[slot, 0], NN) + dot32(d_up, w_buf[slot, 1], NN)

    for s in range(2, slices):

        @pl.when(step == s)
        def _(s=s):
            for copy in pieces(d_out[s - 2], s - 2, d_buf, d_sem, True):
                copy.wait()

    d_buf[slot, 2] = dot32(hidden, g, TN).astype(jnp.bfloat16)
    d_buf[slot, 0] = dot32(d_gate, n, TN).astype(jnp.bfloat16)
    d_buf[slot, 1] = dot32(d_up, n, TN).astype(jnp.bfloat16)

    for s in range(slices):

        @pl.when(step == s)
        def _(s=s):
            for copy in pieces(d_out[s], s, d_buf, d_sem, True):
                copy.start()
            if s + 2 < slices:
                for copy in pieces(w_in[s + 2], s + 2, w_buf, w_sem, False):
                    copy.start()
            if s == slices - 1:
                for last in range(max(0, slices - 2), slices):
                    for copy in pieces(d_out[last], last, d_buf, d_sem, True):
                        copy.wait()


def feed(n, g, weights, spots):
    slices = len(weights)
    rows, width = n.shape
    hidden = weights[0][0].shape[1]
    whole = pl.BlockSpec((rows, width), lambda i, *_: (0, 0))
    there = pl.BlockSpec(memory_space=pl.ANY)
    acc = jax.ShapeDtypeStruct((rows, width), jnp.float32)
    part = jax.ShapeDtypeStruct((2, 3, hidden, LANES), jnp.bfloat16)
    found = pl.pallas_call(
        functools.partial(feed_kernel, slices=slices),
        out_shape=(acc, acc) + (part,) * (4 * slices),
        grid_spec=pltpu.PrefetchScalarGridSpec(
            num_scalar_prefetch=1,
            grid=(slices,),
            in_specs=[whole, whole] + [there] * (PIECES * slices),
            out_specs=(whole, whole) + (there,) * (4 * slices),
            scratch_shapes=[
                pltpu.VMEM((2, 3, hidden, width), jnp.bfloat16),
                pltpu.VMEM((2, 3, hidden, width), jnp.bfloat16),
                pltpu.SemaphoreType.DMA((2,)),
                pltpu.SemaphoreType.DMA((2,)),
            ],
        ),
        cost_estimate=pl.CostEstimate(
            flops=27 * slices * rows * hidden * width,
            transcendentals=slices * rows * hidden,
            bytes_accessed=12 * slices * hidden * width + 12 * rows * width,
        ),
        name="feed",
    )(spots, n, g, *[array for slice_ in weights for array in slice_])
    return found[0], found[1], [found[2 + 4 * s : 6 + 4 * s] for s in range(slices)]


def swap_over(axis, count, bit):
    return [(i, i ^ bit) for i in range(count)]


def spots_of(me, chip_bits):
    rows = []
    for first, second in chip_bits:
        rows += [0, first, second, first | second, 1, 1 | first, 1 | second, 1 | first | second]
    return jnp.bitwise_xor(me, jnp.array(rows, jnp.int32))


def after(value, *others):
    return lax.optimization_barrier((value, *others))[0]


def cross_first(piece, count, first, second):
    swap = lambda value, bit: lax.ppermute(value, "dp", swap_over("dp", count, bit))
    return piece, swap(piece, first), swap(piece, second), swap(piece, 1)


def cross_last(found, count, second):
    swap = lambda value, bit: lax.ppermute(value, "dp", swap_over("dp", count, bit))
    own, one, two, core = found
    both = swap(one, second)
    return [own, one, two, both, core, swap(one, 1), swap(two, 1), swap(both, 1)]


def scatter_slice(parts, count, first, second):
    swap = lambda value, bit: lax.ppermute(value, "dp", swap_over("dp", count, bit))
    low = lambda value: value.astype(jnp.bfloat16)
    wide = lambda value: value.astype(jnp.float32)
    away = low(wide(parts[1]) + wide(swap(parts[3], 1)))
    near = wide(parts[0]) + wide(swap(parts[2], 1))
    near = near + wide(swap(away, second))
    return near[0] + wide(swap(low(near[1]), first))


def on_device(
    inputs, cotangent, segment_ids, row_length,
    w_qkv, m_qkv, v_qkv, w_out, m_out, v_out, w_gate_up, m_gate_up, v_gate_up, w_down, m_down, v_down,
    norm_gains, m_gains, v_gains,
    *, dp, mp,
):
    f32, bf16 = jnp.float32, jnp.bfloat16
    z = lax.axis_index("mp")
    me = lax.axis_index("dp")
    onward = [(i, (i + 1) % mp) for i in range(mp)]
    ring = lambda value: lax.ppermute(value, "mp", onward)
    rows, width = inputs.shape[1:]
    seq_len = segment_ids.shape[1]
    hidden_here = w_down.shape[0]
    lanes_here = w_down.shape[1]
    heads_width = w_out.shape[0]
    exchange = dp == PIECES and lanes_here == LANES

    groups = 2 if heads_width % (4 * HEAD) == 0 else 1
    share = heads_width // groups

    seg_row = segment_ids[0]
    live_row = jnp.arange(seq_len, dtype=jnp.int32) < row_length[0]
    live = live_row.astype(f32)[:, None]

    wide, narrow = min(1024, seq_len), min(512, seq_len)
    lo, hi = key_blocks(seg_row, row_length[0], wide, narrow)
    lo_back, hi_back = key_blocks(seg_row, row_length[0], narrow, narrow)

    copy_qkv = w_qkv.astype(bf16).reshape(3, lanes_here, groups, share).transpose(2, 0, 3, 1).reshape(3 * heads_width, lanes_here)
    copy_out = w_out.astype(bf16)
    copy_feed = jnp.concatenate([w_gate_up.astype(bf16).transpose(0, 2, 1), w_down.astype(bf16)[None]])
    copy_gains = jnp.pad(norm_gains.astype(bf16), ((0, 14), (0, 0)))
    chip_bits = [(2, 4) if s % 2 == 0 or not exchange else (4, 2) for s in range(mp)]
    spots = spots_of(me if exchange else 0, chip_bits)

    def start_cross(piece, s):
        if exchange:
            return cross_first(piece, dp, *chip_bits[s])
        return lax.all_gather(piece, "dp", axis=2, tiled=True)

    def end_cross(found, s):
        if exchange:
            return cross_last(found, dp, chip_bits[s][1])
        whole = found.reshape(3, hidden_here, PIECES, LANES)
        return [whole[:, :, block] for block in (0, 2, 4, 6, 1, 3, 5, 7)]

    feed_own = [copy_feed, ring(copy_feed)]
    blocks = [inputs[0]]
    for _ in range(mp - 1):
        blocks.append(ring(blocks[-1]))
    full_first = lax.all_gather(jnp.concatenate([copy_qkv, copy_gains]), "dp", axis=1, tiled=True)
    full_qkv = full_first[: 3 * heads_width]
    gain_one = full_first[3 * heads_width].astype(f32)
    gain_two = full_first[3 * heads_width + 1].astype(f32)
    full_out = lax.all_gather(copy_out, ("dp", "mp"), axis=0).reshape(dp, mp, groups, share, lanes_here)
    full_out = [full_out[:, :, i].transpose(1, 2, 0, 3).reshape(mp * share, width) for i in range(groups)]
    feed_full = [end_cross(start_cross(feed_own[s], s), s) for s in range(2)]

    resid_in = inputs[0].astype(f32)
    scale_one = rms_scale(resid_in)
    hat_one = resid_in * scale_one
    hats = []
    normed_one = jnp.zeros((seq_len, width), bf16)
    for s, block in enumerate(blocks):
        block = block.astype(f32)
        hats.append(block * rms_scale(block))
        at = lax.rem(z + mp - s, mp) * rows
        normed_one = lax.dynamic_update_slice(normed_one, (hats[-1] * gain_one).astype(bf16), (at, 0))
    qkv = dot32(normed_one, full_qkv, NT).astype(bf16)

    pending = ring(after(feed_own[1], blocks[-1]))
    crossing = []
    raw_out, log_sums, attended = [], [], []
    for i in range(groups):
        raw, logs = attend(qkv, i, share, seg_row, lo, hi, wide, narrow)
        raw_out.append(raw)
        log_sums.append(jnp.where(live_row[None, :], logs, -NEG_FILL))
        mine = (raw * live).astype(bf16)
        pending, mine = lax.optimization_barrier((pending, mine))
        feed_own.append(pending)
        crossing.append(start_cross(pending, len(feed_own) - 1))
        if len(feed_own) < mp:
            pending = ring(pending)
        attended.append(lax.all_to_all(mine, "mp", split_axis=0, concat_axis=1, tiled=True))
    while len(feed_own) < mp:
        feed_own.append(pending)
        crossing.append(start_cross(pending, len(feed_own) - 1))
        pending = ring(pending)
    feed_full += [end_cross(found, s + 2) for s, found in enumerate(crossing)]

    after_attn = resid_in
    for part, weight in zip(attended, full_out):
        after_attn = after_attn + dot32(part, weight, NN)
    scale_two = rms_scale(after_attn)
    hat_two = after_attn * scale_two
    normed_two = (hat_two * gain_two).astype(bf16)

    fed, d_normed_two, d_feed = [], [], []
    for start in range(0, mp, 2):
        stop = min(start + 2, mp)
        out_part, d_part, grads = feed(
            normed_two, cotangent[0], feed_full[start:stop], spots[PIECES * start : PIECES * stop]
        )
        fed.append(out_part)
        d_normed_two.append(d_part)
        d_feed += grads
    d_normed_two = functools.reduce(jnp.add, d_normed_two)
    d_after = cotangent[0].astype(f32) + norm_back(d_normed_two, hat_two, scale_two, gain_two)

    d_branch = d_after.astype(bf16)
    d_attended = [
        lax.all_to_all(dot32(d_branch, weight, NT).astype(bf16), "mp", split_axis=1, concat_axis=0, tiled=True)
        for weight in full_out
    ]
    grad_out = [dot32(part, d_branch, TN).astype(bf16).reshape(mp, share, width) for part in attended]
    grad_out = jnp.stack(grad_out, axis=1).reshape(mp * heads_width, width)
    grad_out = lax.psum_scatter(grad_out, "dp", scatter_dimension=1, tiled=True)
    grad_out = lax.psum_scatter(grad_out, "mp", scatter_dimension=0, tiled=True).astype(f32)

    d_qkv = []
    for i in range(groups):
        d_here = jnp.where(live_row[:, None], d_attended[i], jnp.zeros((), bf16))
        row_dot = jnp.sum((raw_out[i] * d_here).reshape(seq_len, share // HEAD, HEAD), axis=-1).T
        d_qkv.append(attend_back(qkv, i, d_here, log_sums[i], row_dot, seg_row, lo_back, hi_back, narrow, narrow))
    d_qkv = jnp.concatenate(d_qkv, axis=1)
    block_output = after_attn + functools.reduce(jnp.add, fed)
    grad_gain_two = jnp.sum(d_normed_two * hat_two, axis=0)

    total = None
    grad_gain_one = jnp.zeros((width,), f32)
    for s in [*range(1, mp), 0]:
        at = lax.rem(z + mp - s, mp) * rows
        part = dot32(lax.dynamic_slice(d_qkv, (at, 0), (rows, d_qkv.shape[1])), full_qkv, NN)
        grad_gain_one = grad_gain_one + jnp.sum(part * hats[s], axis=0)
        total = part if total is None else ring(total.astype(bf16)).astype(f32) + part
    d_normed_one = total
    input_grad = d_after + norm_back(d_normed_one, hat_one, scale_one, gain_one)

    grad_qkv = dot32(d_qkv, normed_one, TN).astype(bf16)
    grad_qkv = lax.psum_scatter(grad_qkv, "dp", scatter_dimension=1, tiled=True).astype(f32)
    grad_qkv = grad_qkv.reshape(groups, 3, share, lanes_here).transpose(1, 3, 0, 2).reshape(w_qkv.shape)

    if exchange:
        owned = [scatter_slice(parts, dp, *bits) for parts, bits in zip(d_feed, chip_bits)]
    else:
        back = jnp.array([0, 4, 1, 5, 2, 6, 3, 7])
        owned = []
        for parts in d_feed:
            whole = jnp.concatenate(parts)[back].transpose(1, 2, 0, 3).reshape(3, hidden_here, width)
            owned.append(lax.psum_scatter(whole, "dp", scatter_dimension=2, tiled=True).astype(f32))
    total = owned[1]
    for s in [*range(2, mp), 0]:
        total = ring(total.astype(bf16)).astype(f32) + owned[s]
    grad_gate_up = total[:2].transpose(0, 2, 1)
    grad_down = total[2]

    grad_gains = jnp.stack([grad_gain_one, grad_gain_two])
    for axis, count in (("mp", mp), ("dp", dp)):
        bit = 1
        while bit < count:
            grad_gains = grad_gains + lax.ppermute(grad_gains, axis, swap_over(axis, count, bit))
            bit *= 2
    grad_gains = lax.dynamic_slice(grad_gains, (0, me * lanes_here), (2, lanes_here))

    new_qkv = adam_update(w_qkv, m_qkv, v_qkv, grad_qkv, RATES[0], DECAY_RATE)
    new_out = adam_update(w_out, m_out, v_out, grad_out, RATES[1], DECAY_RATE)
    new_gate_up = adam_update(w_gate_up, m_gate_up, v_gate_up, grad_gate_up, RATES[2], DECAY_RATE)
    new_down = adam_update(w_down, m_down, v_down, grad_down, RATES[3], DECAY_RATE)
    new_gains = adam_update(norm_gains, m_gains, v_gains, grad_gains, RATES[4], 0.0)
    return (block_output[None], input_grad[None], *new_qkv, *new_out, *new_gate_up, *new_down, *new_gains)


def solution(mesh):
    tokens = P("dp", "mp", None)
    stacked = P(None, "dp", "mp")
    flat = P("mp", "dp")
    gains = P(None, "dp")
    return jax.shard_map(
        functools.partial(on_device, dp=mesh.shape["dp"], mp=mesh.shape["mp"]),
        mesh=mesh,
        in_specs=(tokens, tokens, P("dp", None), P("dp"))
        + (stacked,) * 3 + (flat,) * 3 + (stacked,) * 3 + (flat,) * 3 + (gains,) * 3,
        out_specs=(tokens, tokens) + (stacked,) * 4 + (flat,) * 4 + (stacked,) * 4 + (flat,) * 4 + (gains,) * 4,
        check_vma=False,
    )
```

```python
import functools
import math

import jax
import jax.numpy as jnp
from jax import lax
from jax.experimental import pallas as pl
from jax.experimental.pallas import tpu as pltpu
from jax.sharding import PartitionSpec as P

HEAD = 64
ADAM_STEP = 5
LANES = 128


EPS_NORM = 1e-06
BETA_ONE = 0.9
BETA_TWO = 0.999
ADAM_EPS = 1e-08
DECAY_RATE = 0.1
RATES = (0.03, 0.5, 0.06, 0.04, 0.4)
NEG_FILL = -1e30
GELU_IN = 0.7978845608028654
GELU_CUBE = 0.044715


def rms_scale(values_in):
    return lax.rsqrt(jnp.mean(values_in * values_in, axis=-1, keepdims=True) + EPS_NORM)


def norm_back(d_normed, hat, scale, gain):
    scaled = gain * d_normed
    return scale * (scaled - hat * jnp.mean(scaled * hat, axis=-1, keepdims=True))


def adam_update(weight, moment, second, grad, step_rate, decay):
    moment_new = BETA_ONE * moment + (1.0 - BETA_ONE) * grad
    second_new = BETA_TWO * second + (1.0 - BETA_TWO) * grad * grad
    moment_hat = moment_new / (1.0 - BETA_ONE**ADAM_STEP)
    second_hat = second_new / (1.0 - BETA_TWO**ADAM_STEP)
    updated = weight - step_rate * (moment_hat / (jnp.sqrt(second_hat) + ADAM_EPS) + decay * weight)
    return (updated, updated.astype(jnp.bfloat16), moment_new, second_new)


NT = (((1,), (1,)), ((), ()))
NN = (((1,), (0,)), ((), ()))


def dot32(left, right, dims):
    return lax.dot_general(left, right, dims, preferred_element_type=jnp.float32)


def attend_kernel(lo_ref, hi_ref, q_ref, k_ref, v_ref, seg_q, seg_k, o_ref, lse_ref, vt_ref, *, bk, heads):
    i = pl.program_id(0)
    bq = q_ref.shape[0]

    @pl.when(i == 0)
    def _():
        vt_ref[...] = v_ref[...].T

    def body(j, carry):
        ks = pl.ds(pl.multiple_of(j * bk, bk), bk)
        same = seg_k[ks, :] == seg_q[...]
        out = []
        for h in range(heads):
            peak, total, acc = carry[h]
            hs = slice(h * HEAD, (h + 1) * HEAD)
            s = jnp.where(same, dot32(k_ref[ks, hs], q_ref[:, hs], NT), NEG_FILL)
            peak_new = jnp.maximum(peak, jnp.max(s, axis=0, keepdims=True))
            p = jnp.exp(s - peak_new)
            keep = jnp.exp(peak - peak_new)
            total = total * keep + jnp.sum(p, axis=0, keepdims=True)
            acc = acc * keep + dot32(vt_ref[hs, ks], p.astype(jnp.bfloat16), NN)
            out.append((peak_new, total, acc))
        return tuple(out)

    first = tuple(
        (
            jnp.full((1, bq), NEG_FILL, jnp.float32),
            jnp.zeros((1, bq), jnp.float32),
            jnp.zeros((HEAD, bq), jnp.float32),
        )
        for _ in range(heads)
    )
    found = lax.fori_loop(lo_ref[i], hi_ref[i], body, first)
    totals = [jnp.where(total > 0, total, 1.0) for _, total, _ in found]
    o_ref[...] = jnp.concatenate([acc / t for (_, _, acc), t in zip(found, totals)], axis=0).T
    lse_ref[...] = jnp.concatenate([peak + jnp.log(t) for (peak, _, _), t in zip(found, totals)], axis=0)


def attend(qkv, group, width, seg, lo, hi, bq, bk):
    rows = qkv.shape[0]
    heads = width // HEAD
    return pl.pallas_call(
        functools.partial(attend_kernel, bk=bk, heads=heads),
        out_shape=(
            jax.ShapeDtypeStruct((rows, width), jnp.float32),
            jax.ShapeDtypeStruct((heads, rows), jnp.float32),
        ),
        grid_spec=pltpu.PrefetchScalarGridSpec(
            num_scalar_prefetch=2,
            grid=(rows // bq,),
            in_specs=[
                pl.BlockSpec((bq, width), lambda i, *_: (i, 3 * group)),
                pl.BlockSpec((rows, width), lambda i, *_: (0, 3 * group + 1)),
                pl.BlockSpec((rows, width), lambda i, *_: (0, 3 * group + 2)),
                pl.BlockSpec((1, bq), lambda i, *_: (0, i)),
                pl.BlockSpec((rows, 1), lambda i, *_: (0, 0)),
            ],
            out_specs=(
                pl.BlockSpec((bq, width), lambda i, *_: (i, 0)),
                pl.BlockSpec((heads, bq), lambda i, *_: (0, i)),
            ),
            scratch_shapes=[pltpu.VMEM((width, rows), jnp.bfloat16)],
        ),
        cost_estimate=pl.CostEstimate(
            flops=16 * heads * rows * rows * HEAD, transcendentals=heads * rows * rows, bytes_accessed=10 * rows * width
        ),
        name="attend",
    )(lo, hi, qkv, qkv, qkv, seg[None, :], seg[:, None])


def attend_back_kernel(
    lo_ref, hi_ref, q_ref, do_ref, lse_ref, dot_ref, k_ref, v_ref, seg_q, seg_k,
    d_ref, dk_sum, dv_sum, kt_ref, *, bk, heads,
):
    i = pl.program_id(0)
    bq, width = q_ref.shape

    @pl.when(i == 0)
    def _():
        kt_ref[...] = k_ref[...].T
        dk_sum[...] = jnp.zeros_like(dk_sum)
        dv_sum[...] = jnp.zeros_like(dv_sum)

    def body(j, carry):
        ks = pl.ds(pl.multiple_of(j * bk, bk), bk)
        same = seg_k[ks, :] == seg_q[...]
        out, dks, dvs = [], [], []
        for h in range(heads):
            hs = slice(h * HEAD, (h + 1) * HEAD)
            qh = q_ref[:, hs]
            doh = do_ref[:, hs]
            s = dot32(k_ref[ks, hs], qh, NT)
            p = jnp.exp(jnp.where(same, s - lse_ref[h : h + 1, :], NEG_FILL))
            dp = dot32(v_ref[ks, hs], doh, NT)
            ds = (p * (dp - dot_ref[h : h + 1, :])).astype(jnp.bfloat16)
            dvs.append(dot32(p.astype(jnp.bfloat16), doh, NN))
            dks.append(dot32(ds, qh, NN))
            out.append(carry[h] + dot32(kt_ref[hs, ks], ds, NN))
        dk_sum[ks, :] += jnp.concatenate(dks, axis=1)
        dv_sum[ks, :] += jnp.concatenate(dvs, axis=1)
        return tuple(out)

    first = tuple(jnp.zeros((HEAD, bq), jnp.float32) for _ in range(heads))
    found = lax.fori_loop(lo_ref[i], hi_ref[i], body, first)
    d_ref[pl.ds(pl.multiple_of(i * bq, bq), bq), :width] = jnp.concatenate(found, axis=0).T.astype(d_ref.dtype)

    @pl.when(i == pl.num_programs(0) - 1)
    def _():
        d_ref[:, width : 2 * width] = dk_sum[...].astype(d_ref.dtype)
        d_ref[:, 2 * width :] = dv_sum[...].astype(d_ref.dtype)


def attend_back(qkv, group, d_out, lse, row_dot, seg, lo, hi, bq, bk):
    rows, width = d_out.shape
    heads = width // HEAD
    by_row = lambda i, *_: (i, 0)
    by_col = lambda i, *_: (0, i)
    return pl.pallas_call(
        functools.partial(attend_back_kernel, bk=bk, heads=heads),
        out_shape=jax.ShapeDtypeStruct((rows, 3 * width), jnp.bfloat16),
        grid_spec=pltpu.PrefetchScalarGridSpec(
            num_scalar_prefetch=2,
            grid=(rows // bq,),
            in_specs=[
                pl.BlockSpec((bq, width), lambda i, *_: (i, 3 * group)),
                pl.BlockSpec((bq, width), by_row),
                pl.BlockSpec((heads, bq), by_col),
                pl.BlockSpec((heads, bq), by_col),
                pl.BlockSpec((rows, width), lambda i, *_: (0, 3 * group + 1)),
                pl.BlockSpec((rows, width), lambda i, *_: (0, 3 * group + 2)),
                pl.BlockSpec((1, bq), by_col),
                pl.BlockSpec((rows, 1), lambda i, *_: (0, 0)),
            ],
            out_specs=pl.BlockSpec((rows, 3 * width), lambda i, *_: (0, 0)),
            scratch_shapes=[
                pltpu.VMEM((rows, width), jnp.float32),
                pltpu.VMEM((rows, width), jnp.float32),
                pltpu.VMEM((width, rows), jnp.bfloat16),
            ],
        ),
        cost_estimate=pl.CostEstimate(
            flops=40 * heads * rows * rows * HEAD, transcendentals=heads * rows * rows, bytes_accessed=16 * rows * width
        ),
        name="attend_back",
    )(lo, hi, qkv, d_out, lse, row_dot, qkv, qkv, seg[None, :], seg[:, None])


def key_blocks(seg, length, bq, bk):
    lo = jnp.sum(seg[None, :] < seg[::bq][:, None], axis=1)
    hi = jnp.minimum(jnp.sum(seg[None, :] <= seg[bq - 1 :: bq][:, None], axis=1), length)
    lo = lo // bk
    hi = (hi + bk - 1) // bk
    dead = jnp.arange(seg.shape[0] // bq) * bq >= length
    return lo.astype(jnp.int32), jnp.where(dead, lo, hi).astype(jnp.int32)


TN = (((0,), (0,)), ((), ()))
PIECES = 8


def feed_kernel(spots, *refs, slices):
    n_ref, g_ref = refs[:2]
    w_in = [refs[2 + PIECES * s : 2 + PIECES * (s + 1)] for s in range(slices)]
    at = 2 + PIECES * slices
    out_ref, dn_ref = refs[at : at + 2]
    d_out = [refs[at + 2 + 4 * s : at + 6 + 4 * s] for s in range(slices)]
    w_buf, d_buf, w_sem, d_sem = refs[at + 2 + 4 * slices :]
    step = pl.program_id(0)
    slot = lax.rem(step, 2)

    def pieces(arrays, s, buf, sem, outward):
        held = s % 2
        for p in range(PIECES):
            lanes = pl.ds(pl.multiple_of(spots[s * PIECES + p] * LANES, LANES), LANES)
            near = buf.at[held, :, :, lanes]
            src, dst = (near, arrays[p // 2].at[p % 2]) if outward else (arrays[p], near)
            yield pltpu.make_async_copy(src, dst, sem.at[held])

    for s in range(slices):

        @pl.when(step == s)
        def _(s=s):
            if s == 0:
                for first in range(min(2, slices)):
                    for copy in pieces(w_in[first], first, w_buf, w_sem, False):
                        copy.start()
            for copy in pieces(w_in[s], s, w_buf, w_sem, False):
                copy.wait()

    @pl.when(step == 0)
    def _():
        out_ref[...] = jnp.zeros_like(out_ref)
        dn_ref[...] = jnp.zeros_like(dn_ref)

    n = n_ref[...]
    g = g_ref[...]
    gate = dot32(n, w_buf[slot, 0], NT)
    up = dot32(n, w_buf[slot, 1], NT)
    d_hidden = dot32(g, w_buf[slot, 2], NT)
    square = gate * gate
    bent = jnp.tanh(gate * (GELU_IN + (GELU_IN * GELU_CUBE) * square))
    half = 0.5 + 0.5 * bent
    lifted = gate * half
    slope = half + (0.5 * gate) * (1.0 - bent * bent) * (GELU_IN + (3.0 * GELU_IN * GELU_CUBE) * square)
    hidden = (lifted * up).astype(jnp.bfloat16)
    d_gate = (d_hidden * up * slope).astype(jnp.bfloat16)
    d_up = (d_hidden * lifted).astype(jnp.bfloat16)
    out_ref[...] += dot32(hidden, w_buf[slot, 2], NN)
    dn_ref[...] += dot32(d_gate, w_buf[slot, 0], NN) + dot32(d_up, w_buf[slot, 1], NN)

    for s in range(2, slices):

        @pl.when(step == s)
        def _(s=s):
            for copy in pieces(d_out[s - 2], s - 2, d_buf, d_sem, True):
                copy.wait()

    d_buf[slot, 2] = dot32(hidden, g, TN).astype(jnp.bfloat16)
    d_buf[slot, 0] = dot32(d_gate, n, TN).astype(jnp.bfloat16)
    d_buf[slot, 1] = dot32(d_up, n, TN).astype(jnp.bfloat16)

    for s in range(slices):

        @pl.when(step == s)
        def _(s=s):
            for copy in pieces(d_out[s], s, d_buf, d_sem, True):
                copy.start()
            if s + 2 < slices:
                for copy in pieces(w_in[s + 2], s + 2, w_buf, w_sem, False):
                    copy.start()
            if s == slices - 1:
                for last in range(max(0, slices - 2), slices):
                    for copy in pieces(d_out[last], last, d_buf, d_sem, True):
                        copy.wait()


def feed(n, g, weights, spots):
    slices = len(weights)
    rows, width = n.shape
    hidden = weights[0][0].shape[1]
    whole = pl.BlockSpec((rows, width), lambda i, *_: (0, 0))
    there = pl.BlockSpec(memory_space=pl.ANY)
    acc = jax.ShapeDtypeStruct((rows, width), jnp.float32)
    part = jax.ShapeDtypeStruct((2, 3, hidden, LANES), jnp.bfloat16)
    found = pl.pallas_call(
        functools.partial(feed_kernel, slices=slices),
        out_shape=(acc, acc) + (part,) * (4 * slices),
        grid_spec=pltpu.PrefetchScalarGridSpec(
            num_scalar_prefetch=1,
            grid=(slices,),
            in_specs=[whole, whole] + [there] * (PIECES * slices),
            out_specs=(whole, whole) + (there,) * (4 * slices),
            scratch_shapes=[
                pltpu.VMEM((2, 3, hidden, width), jnp.bfloat16),
                pltpu.VMEM((2, 3, hidden, width), jnp.bfloat16),
                pltpu.SemaphoreType.DMA((2,)),
                pltpu.SemaphoreType.DMA((2,)),
            ],
        ),
        cost_estimate=pl.CostEstimate(
            flops=27 * slices * rows * hidden * width,
            transcendentals=slices * rows * hidden,
            bytes_accessed=12 * slices * hidden * width + 12 * rows * width,
        ),
        name="feed",
    )(spots, n, g, *[array for slice_ in weights for array in slice_])
    return found[0], found[1], [found[2 + 4 * s : 6 + 4 * s] for s in range(slices)]


def swap_over(axis, count, bit):
    return [(i, i ^ bit) for i in range(count)]


def spots_of(me, chip_bits):
    rows = []
    for first, second in chip_bits:
        rows += [0, first, second, first | second, 1, 1 | first, 1 | second, 1 | first | second]
    return jnp.bitwise_xor(me, jnp.array(rows, jnp.int32))


def after(value, *others):
    return lax.optimization_barrier((value, *others))[0]


def cross_first(piece, count, first, second):
    swap = lambda value, bit: lax.ppermute(value, "dp", swap_over("dp", count, bit))
    return piece, swap(piece, first), swap(piece, second), swap(piece, 1)


def cross_last(found, count, second):
    swap = lambda value, bit: lax.ppermute(value, "dp", swap_over("dp", count, bit))
    own, one, two, core = found
    both = swap(one, second)
    return [own, one, two, both, core, swap(one, 1), swap(two, 1), swap(both, 1)]


def scatter_slice(parts, count, first, second):
    swap = lambda value, bit: lax.ppermute(value, "dp", swap_over("dp", count, bit))
    low = lambda value: value.astype(jnp.bfloat16)
    wide = lambda value: value.astype(jnp.float32)
    away = low(wide(parts[1]) + wide(swap(parts[3], 1)))
    near = wide(parts[0]) + wide(swap(parts[2], 1))
    near = near + wide(swap(away, second))
    return near[0] + wide(swap(low(near[1]), first))


def join_kernel(spots, *refs, count, sets, high):
    pieces, whole, sem = refs[:count], refs[count], refs[count + 1]
    copies = []
    for k in range(count):
        for s in range(sets):
            lanes = pl.ds(pl.multiple_of(spots[k] * LANES, LANES), LANES)
            rows = pl.ds(pl.multiple_of(spots[count + s] * high, high), high)
            copies.append(pltpu.make_async_copy(pieces[k].at[s], whole.at[rows, lanes], sem))
    for copy in copies:
        copy.start()
    for copy in copies:
        copy.wait()


def part_kernel(spots, whole, *refs, count, sets, high):
    pieces, sem = refs[:count], refs[count]
    copies = []
    for k in range(count):
        for s in range(sets):
            lanes = pl.ds(pl.multiple_of(spots[k] * LANES, LANES), LANES)
            rows = pl.ds(pl.multiple_of(spots[count + s] * high, high), high)
            copies.append(pltpu.make_async_copy(whole.at[rows, lanes], pieces[k].at[s], sem))
    for copy in copies:
        copy.start()
    for copy in copies:
        copy.wait()


def join(pieces, spots):
    count = len(pieces)
    sets, high, _ = pieces[0].shape
    shape = (sets * high, count * LANES)
    return pl.pallas_call(
        functools.partial(join_kernel, count=count, sets=sets, high=high),
        out_shape=jax.ShapeDtypeStruct(shape, pieces[0].dtype),
        grid_spec=pltpu.PrefetchScalarGridSpec(
            num_scalar_prefetch=1,
            grid=(1,),
            in_specs=[pl.BlockSpec(memory_space=pl.ANY)] * count,
            out_specs=pl.BlockSpec(shape, lambda i, *_: (0, 0)),
            scratch_shapes=[pltpu.SemaphoreType.DMA],
        ),
        name="join",
    )(spots, *pieces)


def part(whole, spots, sets):
    high = whole.shape[0] // sets
    count = whole.shape[1] // LANES
    there = pl.BlockSpec(memory_space=pl.ANY)
    return pl.pallas_call(
        functools.partial(part_kernel, count=count, sets=sets, high=high),
        out_shape=(jax.ShapeDtypeStruct((sets, high, LANES), whole.dtype),) * count,
        grid_spec=pltpu.PrefetchScalarGridSpec(
            num_scalar_prefetch=1,
            grid=(1,),
            in_specs=[pl.BlockSpec(whole.shape, lambda i, *_: (0, 0))],
            out_specs=(there,) * count,
            scratch_shapes=[pltpu.SemaphoreType.DMA],
        ),
        name="part",
    )(spots, whole)


def on_device(
    inputs, cotangent, segment_ids, row_length,
    w_qkv, m_qkv, v_qkv, w_out, m_out, v_out, w_gate_up, m_gate_up, v_gate_up, w_down, m_down, v_down,
    norm_gains, m_gains, v_gains,
    *, dp, mp,
):
    f32, bf16 = jnp.float32, jnp.bfloat16
    low = lambda value: value.astype(bf16)
    wide_of = lambda value: value.astype(f32)
    z = lax.axis_index("mp")
    me = lax.axis_index("dp")
    core = lax.rem(me, 2)
    rows, width = inputs.shape[1:]
    seq_len = segment_ids.shape[1]
    hidden_here = w_down.shape[0]
    lanes_here = w_down.shape[1]
    heads_width = w_out.shape[0]
    exchange = dp == PIECES and lanes_here == LANES
    half = rows // 2
    parts_of_heads = 2
    share = heads_width // parts_of_heads

    swap = lambda value, bit: lax.ppermute(value, "dp", swap_over("dp", dp, bit))
    pair = lambda value: swap(value, 1)
    line = lambda value, pairs: lax.ppermute(value, "mp", pairs)
    onward = lambda value: line(value, [(i, (i + 1) % mp) for i in range(mp)])
    backward = lambda value: line(value, [(i, (i - 1) % mp) for i in range(mp)])
    across = lambda value: line(value, swap_over("mp", mp, 2))
    tie = lax.optimization_barrier

    home = z // 2
    outer = (z == 0) | (z == mp - 1)
    first = core == 0

    copy_qkv = low(w_qkv).reshape(3, lanes_here, parts_of_heads, share).transpose(2, 0, 3, 1)
    copy_qkv = copy_qkv.reshape(3 * heads_width, lanes_here)
    copy_first = jnp.concatenate([copy_qkv, jnp.pad(low(norm_gains), ((0, 14), (0, 0)))])
    copy_out = low(w_out)
    copy_feed = jnp.concatenate([low(w_gate_up).transpose(0, 2, 1), low(w_down)[None]])
    chip_bits = [(2, 4) if s % 2 == 0 or not exchange else (4, 2) for s in range(mp)]
    spots = spots_of(me if exchange else 0, chip_bits)

    def start_cross(piece, s):
        if exchange:
            return cross_first(piece, dp, *chip_bits[s])
        return lax.all_gather(piece, "dp", axis=2, tiled=True)

    def end_cross(found, s):
        if exchange:
            return cross_last(found, dp, chip_bits[s][1])
        whole = found.reshape(3, hidden_here, PIECES, LANES)
        return [whole[:, :, block] for block in (0, 2, 4, 6, 1, 3, 5, 7)]

    far_first = across(copy_first)

    x_own = inputs[0]
    keep = lax.dynamic_slice(x_own, (core * half, 0), (half, width))
    got = pair(lax.dynamic_slice(x_own, ((1 - core) * half, 0), (half, width)))
    ids = jnp.concatenate([segment_ids[0], jnp.broadcast_to(row_length, (LANES,))])
    ids = jnp.where(home == core, ids, pair(ids))
    row_a = jnp.where(first, keep, got)
    row_b = jnp.where(first, got, keep)
    down_one = line(row_a, [(3, 2), (2, 1), (1, 0)])
    up_one = line(row_b, [(0, 1), (1, 2), (2, 3)])
    down_two = line(down_one, [(2, 1), (1, 0)])
    up_two = line(up_one, [(1, 2), (2, 3)])
    side = line(after(jnp.where(z == 0, row_a, row_b), down_one, up_one), [(0, 1), (3, 2)])
    far = line(jnp.where(z == 1, down_two, up_two), [(1, 0), (2, 3)])
    held = [
        (jnp.where(home == 0, row_a, row_b), z),
        (jnp.where(z == 0, down_one, jnp.where(z == 3, up_one, side)), z ^ 1),
        (jnp.where(outer, jnp.where(z == 0, down_two, up_two), jnp.where(z == 1, down_one, up_one)), 2 - home),
        (jnp.where(outer, far, jnp.where(z == 1, down_two, up_two)), 3 * (1 - home)),
    ]

    if exchange:
        two = [jnp.where(first, copy_first, far_first), pair(jnp.where(first, far_first, copy_first))]
        two = jnp.stack(two)
        four = swap(two, 2)
        last_four = swap(jnp.stack([two, four]), 4)
        spots_first = jnp.concatenate([me ^ jnp.arange(PIECES, dtype=jnp.int32), jnp.zeros((1,), jnp.int32)])
        pieces = [two[:1], two[1:], four[:1], four[1:]]
        pieces += [last_four[i, j : j + 1] for i in range(2) for j in range(2)]
        full_first = join(pieces, spots_first)
    else:
        full_first = lax.all_gather(jnp.stack([copy_first, far_first]), "dp", axis=2, tiled=True)
        full_first = jnp.where(first, full_first[0], full_first[1])
    full_qkv = full_first[: 3 * heads_width]
    gain_one = wide_of(full_first[3 * heads_width])
    gain_two = wide_of(full_first[3 * heads_width + 1])

    crossing = [start_cross(copy_feed, 0)]
    if exchange:
        out_one = onward(copy_out)
        out_all = jnp.stack([copy_out, out_one, onward(out_one), backward(copy_out)])
    seg_row = ids[:seq_len]
    length = ids[seq_len]
    live_row = jnp.arange(seq_len, dtype=jnp.int32) < length
    live = wide_of(live_row)[:, None]
    wide, narrow = min(1024, seq_len), min(512, seq_len)
    lo, hi = key_blocks(seg_row, length, wide, narrow)
    lo_back, hi_back = key_blocks(seg_row, length, narrow, narrow)

    hats = []
    normed_one = jnp.zeros((seq_len, width), bf16)
    for value, block in held:
        for piece, side_of in ((value, core), (pair(value), 1 - core)):
            piece = wide_of(piece)
            hats.append(piece * rms_scale(piece))
            at = block * rows + side_of * half
            normed_one = lax.dynamic_update_slice(normed_one, low(hats[-1] * gain_one), (at, 0))
    qkv = low(dot32(normed_one, full_qkv, NT))

    feed_in = after(copy_feed, far)
    plus = onward(feed_in)
    minus = backward(feed_in)
    if exchange:
        out_in = after(out_all, last_four)
        out_two = [out_in, swap(out_in, 2)]
        out_four = out_two + [swap(value, 4) for value in out_two]

    rank = 2 * lax.rem(z, 2) + core

    def column_pairs(s):
        found = []
        for d in range(dp):
            for c in range(mp):
                to_dp = (d // 2) * 2 + c // 2
                to_z = (2 * (c % 2) + d % 2) ^ s
                found.append((d * mp + c, to_dp * mp + to_z))
        return found

    def group_at(s):
        place = z ^ s
        return (2 * core + place // 2) ^ (2 * lax.rem(place, 2))

    def spread(value):
        return [
            lax.ppermute(lax.dynamic_slice(value, ((rank ^ s) * rows, 0), (rows, share)), ("dp", "mp"), column_pairs(s))
            for s in range(mp)
        ]

    def collect(value, i):
        found = jnp.zeros((seq_len, share), value.dtype)
        for s in range(mp):
            piece = lax.dynamic_slice(value, (0, group_at(s) * heads_width + i * share), (rows, share))
            piece = lax.ppermute(piece, ("dp", "mp"), [(there, here) for here, there in column_pairs(s)])
            found = lax.dynamic_update_slice(found, piece, ((rank ^ s) * rows, 0))
        return found

    raw_one, logs_one = attend(qkv, 0, share, seg_row, lo, hi, wide, narrow)
    mine_one = low(raw_one * live)
    if exchange:
        qkv_next, plus, minus, mine_one, *out_four = tie((qkv, plus, minus, mine_one, *out_four))
        out_eight = out_four + [pair(value) for value in out_four]
    else:
        qkv_next, plus, minus, mine_one = tie((qkv, plus, minus, mine_one))
    spread_one = spread(mine_one)
    twice = onward(plus)
    crossing.append(start_cross(plus, 1))
    slice_three = start_cross(minus, 3)
    feed_full = [end_cross(crossing[0], 0)]

    raw_two, logs_two = attend(qkv_next, 1, share, seg_row, lo, hi, wide, narrow)
    mine_two = low(raw_two * live)
    spread_two = spread(mine_two)
    raw_out = [raw_one, raw_two]
    log_sums = [jnp.where(live_row[None, :], logs, -NEG_FILL) for logs in (logs_one, logs_two)]
    feed_full.append(end_cross(crossing[1], 1))
    slice_two = start_cross(twice, 2)

    if exchange:
        place_out = jnp.array([0, 2, 4, 6, 1, 3, 5, 7], jnp.int32)
        spots_out = jnp.concatenate([me ^ place_out, lax.rem(z + mp - jnp.arange(mp, dtype=jnp.int32), mp)])
        full_out = join([out_eight[i] for i in range(PIECES)], spots_out)
    else:
        full_out = lax.all_gather(copy_out, ("dp", "mp"), axis=0)
        full_out = full_out.reshape(dp, mp, heads_width, lanes_here).transpose(1, 2, 0, 3).reshape(mp * heads_width, width)

    attended = jnp.zeros((rows, width), bf16)
    for i, found in enumerate((spread_one, spread_two)):
        for s in range(mp):
            attended = lax.dynamic_update_slice(attended, found[s], (0, group_at(s) * heads_width + i * share))

    resid_in = wide_of(x_own)
    scale_one = rms_scale(resid_in)
    hat_one = resid_in * scale_one
    after_attn = resid_in + dot32(attended, full_out, NN)
    scale_two = rms_scale(after_attn)
    hat_two = after_attn * scale_two
    normed_two = low(hat_two * gain_two)

    fed, d_normed_two, d_feed = [], [], []
    out_part, d_part, grads = feed(normed_two, cotangent[0], feed_full, spots[: 2 * PIECES])
    fed.append(out_part)
    d_normed_two.append(d_part)
    d_feed += grads
    feed_full = [end_cross(slice_two, 2), end_cross(slice_three, 3)]
    out_part, d_part, grads = feed(normed_two, cotangent[0], feed_full, spots[2 * PIECES :])
    fed.append(out_part)
    d_normed_two.append(d_part)
    d_feed += grads
    d_normed_two = functools.reduce(jnp.add, d_normed_two)
    d_after = wide_of(cotangent[0]) + norm_back(d_normed_two, hat_two, scale_two, gain_two)

    d_branch = low(d_after)
    d_attended = low(dot32(d_branch, full_out, NT))
    d_attended = [collect(d_attended, i) for i in range(parts_of_heads)]
    grad_out = low(dot32(attended, d_branch, TN))
    if exchange:
        away = part(grad_out, spots_out, mp)
        near = [low(wide_of(away[k]) + wide_of(pair(away[k + 4]))) for k in range(4)]
        near = [low(wide_of(near[k]) + wide_of(swap(near[k + 2], 4))) for k in range(2)]
        owned_out = wide_of(near[0]) + wide_of(swap(near[1], 2))
        grad_out = wide_of(onward(low(wide_of(onward(low(owned_out[2]))) + owned_out[3])))
        grad_out = grad_out + wide_of(backward(low(owned_out[1]))) + owned_out[0]
    else:
        grad_out = lax.psum_scatter(grad_out, "dp", scatter_dimension=1, tiled=True)
        grad_out = wide_of(lax.psum_scatter(grad_out, "mp", scatter_dimension=0, tiled=True))

    if exchange:
        owned = [scatter_slice(pieces, dp, *bits) for pieces, bits in zip(d_feed, chip_bits)]
    else:
        back = jnp.array([0, 4, 1, 5, 2, 6, 3, 7])
        owned = []
        for pieces in d_feed:
            whole = jnp.concatenate(pieces)[back].transpose(1, 2, 0, 3).reshape(3, hidden_here, width)
            owned.append(wide_of(lax.psum_scatter(whole, "dp", scatter_dimension=2, tiled=True)))
    total = owned[0] + wide_of(backward(low(owned[1])))
    total = total + wide_of(onward(low(owned[3] + wide_of(onward(low(owned[2]))))))
    grad_gate_up = total[:2].transpose(0, 2, 1)
    grad_down = total[2]

    d_qkv = []
    for i in range(parts_of_heads):
        d_here = jnp.where(live_row[:, None], d_attended[i], jnp.zeros((), bf16))
        row_dot = jnp.sum((raw_out[i] * d_here).reshape(seq_len, share // HEAD, HEAD), axis=-1).T
        d_qkv.append(attend_back(qkv, i, d_here, log_sums[i], row_dot, seg_row, lo_back, hi_back, narrow, narrow))
    d_qkv = jnp.concatenate(d_qkv, axis=1)
    block_output = after_attn + functools.reduce(jnp.add, fed)
    grad_gain_two = jnp.sum(d_normed_two * hat_two, axis=0)

    grad_gain_one = jnp.zeros((width,), f32)
    sums = [None] * mp
    for k in range(mp - 1, -1, -1):
        block = held[k][1]
        halves = []
        for j, side_of in enumerate((core, 1 - core)):
            at = block * rows + side_of * half
            found = dot32(lax.dynamic_slice(d_qkv, (at, 0), (half, d_qkv.shape[1])), full_qkv, NN)
            grad_gain_one = grad_gain_one + jnp.sum(found * hats[2 * k + j], axis=0)
            halves.append(found)
        sums[k] = halves[0] + wide_of(pair(low(halves[1])))
    inward = wide_of(line(low(sums[3]), [(0, 1), (3, 2)]))
    passed = low(jnp.where(outer, sums[2], sums[3] + inward))
    up_two = line(passed, [(0, 1), (1, 2)])
    down_two = line(passed, [(3, 2), (2, 1)])
    third = sums[2] + wide_of(jnp.where(z == 1, up_two, down_two))
    up_three = line(jnp.where(z == 2, up_two, low(jnp.where(z == 0, sums[1], third))), [(0, 1), (1, 2), (2, 3)])
    down_three = line(jnp.where(z == 1, down_two, low(jnp.where(z == 3, sums[1], third))), [(3, 2), (2, 1), (1, 0)])
    side = line(low(sums[1]), [(1, 0), (2, 3)])
    mine = sums[0] + wide_of(jnp.where(outer, side, jnp.where(z == 1, up_three, down_three)))
    theirs = wide_of(jnp.where(home == 0, down_three, up_three))
    stay = jnp.where(home == core, mine, theirs)
    moved = wide_of(pair(low(jnp.where(home == core, theirs, mine))))
    d_normed_one = jnp.concatenate([jnp.where(first, stay, moved), jnp.where(first, moved, stay)])
    input_grad = d_after + norm_back(d_normed_one, hat_one, scale_one, gain_one)

    grad_qkv = low(dot32(d_qkv, normed_one, TN))
    if exchange:
        away = part(grad_qkv, spots_first, 1)
        near = [low(wide_of(away[k]) + wide_of(swap(away[k + 4], 4))) for k in range(4)]
        near = [wide_of(near[k]) + wide_of(swap(near[k + 2], 2)) for k in range(2)]
        moved = wide_of(pair(low(near[1][0])))
        stay = near[0][0]
        here = jnp.where(first, stay, moved)
        there = jnp.where(first, moved, stay)
    else:
        nothing = jnp.zeros_like(grad_qkv)
        both = jnp.stack([jnp.where(first, grad_qkv, nothing), jnp.where(first, nothing, grad_qkv)])
        both = wide_of(lax.psum_scatter(both, "dp", scatter_dimension=2, tiled=True))
        here, there = both[0], both[1]
    grad_qkv = here + wide_of(across(low(there)))
    grad_qkv = grad_qkv.reshape(parts_of_heads, 3, share, lanes_here).transpose(1, 3, 0, 2).reshape(w_qkv.shape)

    grad_gains = jnp.stack([grad_gain_one, grad_gain_two])
    for axis, count in (("mp", mp), ("dp", dp)):
        bit = 1
        while bit < count:
            grad_gains = grad_gains + lax.ppermute(grad_gains, axis, swap_over(axis, count, bit))
            bit *= 2
    grad_gains = lax.dynamic_slice(grad_gains, (0, me * lanes_here), (2, lanes_here))

    new_qkv = adam_update(w_qkv, m_qkv, v_qkv, grad_qkv, RATES[0], DECAY_RATE)
    new_out = adam_update(w_out, m_out, v_out, grad_out, RATES[1], DECAY_RATE)
    new_gate_up = adam_update(w_gate_up, m_gate_up, v_gate_up, grad_gate_up, RATES[2], DECAY_RATE)
    new_down = adam_update(w_down, m_down, v_down, grad_down, RATES[3], DECAY_RATE)
    new_gains = adam_update(norm_gains, m_gains, v_gains, grad_gains, RATES[4], 0.0)
    return (block_output[None], input_grad[None], *new_qkv, *new_out, *new_gate_up, *new_down, *new_gains)


def solution(mesh):
    tokens = P("dp", "mp", None)
    stacked = P(None, "dp", "mp")
    flat = P("mp", "dp")
    gains = P(None, "dp")
    return jax.shard_map(
        functools.partial(on_device, dp=mesh.shape["dp"], mp=mesh.shape["mp"]),
        mesh=mesh,
        in_specs=(tokens, tokens, P("dp", None), P("dp"))
        + (stacked,) * 3 + (flat,) * 3 + (stacked,) * 3 + (flat,) * 3 + (gains,) * 3,
        out_specs=(tokens, tokens) + (stacked,) * 4 + (flat,) * 4 + (stacked,) * 4 + (flat,) * 4 + (gains,) * 4,
        check_vma=False,
    )
```

```python
import functools
import math

import jax
import jax.numpy as jnp
from jax import lax
from jax.experimental import pallas as pl
from jax.experimental.pallas import tpu as pltpu
from jax.sharding import PartitionSpec as P

HEAD = 64
ADAM_STEP = 5
LANES = 128


EPS_NORM = 1e-06
BETA_ONE = 0.9
BETA_TWO = 0.999
ADAM_EPS = 1e-08
DECAY_RATE = 0.1
RATES = (0.03, 0.5, 0.06, 0.04, 0.4)
NEG_FILL = -1e30
GELU_IN = 0.7978845608028654
GELU_CUBE = 0.044715


def rms_scale(values_in):
    return lax.rsqrt(jnp.mean(values_in * values_in, axis=-1, keepdims=True) + EPS_NORM)


def norm_back(d_normed, hat, scale, gain):
    scaled = gain * d_normed
    return scale * (scaled - hat * jnp.mean(scaled * hat, axis=-1, keepdims=True))


def adam_update(weight, moment, second, grad, step_rate, decay):
    moment_new = BETA_ONE * moment + (1.0 - BETA_ONE) * grad
    second_new = BETA_TWO * second + (1.0 - BETA_TWO) * grad * grad
    moment_hat = moment_new / (1.0 - BETA_ONE**ADAM_STEP)
    second_hat = second_new / (1.0 - BETA_TWO**ADAM_STEP)
    updated = weight - step_rate * (moment_hat / (jnp.sqrt(second_hat) + ADAM_EPS) + decay * weight)
    return (updated, updated.astype(jnp.bfloat16), moment_new, second_new)


NT = (((1,), (1,)), ((), ()))
NN = (((1,), (0,)), ((), ()))


def dot32(left, right, dims):
    return lax.dot_general(left, right, dims, preferred_element_type=jnp.float32)


def attend_kernel(lo_ref, hi_ref, q_ref, k_ref, v_ref, seg_q, seg_k, o_ref, lse_ref, vt_ref, *, bk, heads):
    i = pl.program_id(0)
    bq = q_ref.shape[0]

    @pl.when(i == 0)
    def _():
        vt_ref[...] = v_ref[...].T

    def body(j, carry):
        ks = pl.ds(pl.multiple_of(j * bk, bk), bk)
        same = seg_k[ks, :] == seg_q[...]
        out = []
        for h in range(heads):
            peak, total, acc = carry[h]
            hs = slice(h * HEAD, (h + 1) * HEAD)
            s = jnp.where(same, dot32(k_ref[ks, hs], q_ref[:, hs], NT), NEG_FILL)
            peak_new = jnp.maximum(peak, jnp.max(s, axis=0, keepdims=True))
            p = jnp.exp(s - peak_new)
            keep = jnp.exp(peak - peak_new)
            total = total * keep + jnp.sum(p, axis=0, keepdims=True)
            acc = acc * keep + dot32(vt_ref[hs, ks], p.astype(jnp.bfloat16), NN)
            out.append((peak_new, total, acc))
        return tuple(out)

    first = tuple(
        (
            jnp.full((1, bq), NEG_FILL, jnp.float32),
            jnp.zeros((1, bq), jnp.float32),
            jnp.zeros((HEAD, bq), jnp.float32),
        )
        for _ in range(heads)
    )
    found = lax.fori_loop(lo_ref[i], hi_ref[i], body, first)
    totals = [jnp.where(total > 0, total, 1.0) for _, total, _ in found]
    o_ref[...] = jnp.concatenate([acc / t for (_, _, acc), t in zip(found, totals)], axis=0).T
    lse_ref[...] = jnp.concatenate([peak + jnp.log(t) for (peak, _, _), t in zip(found, totals)], axis=0)


def attend(qkv, group, width, seg, lo, hi, bq, bk):
    rows = qkv.shape[0]
    heads = width // HEAD
    return pl.pallas_call(
        functools.partial(attend_kernel, bk=bk, heads=heads),
        out_shape=(
            jax.ShapeDtypeStruct((rows, width), jnp.float32),
            jax.ShapeDtypeStruct((heads, rows), jnp.float32),
        ),
        grid_spec=pltpu.PrefetchScalarGridSpec(
            num_scalar_prefetch=2,
            grid=(rows // bq,),
            in_specs=[
                pl.BlockSpec((bq, width), lambda i, *_: (i, 3 * group)),
                pl.BlockSpec((rows, width), lambda i, *_: (0, 3 * group + 1)),
                pl.BlockSpec((rows, width), lambda i, *_: (0, 3 * group + 2)),
                pl.BlockSpec((1, bq), lambda i, *_: (0, i)),
                pl.BlockSpec((rows, 1), lambda i, *_: (0, 0)),
            ],
            out_specs=(
                pl.BlockSpec((bq, width), lambda i, *_: (i, 0)),
                pl.BlockSpec((heads, bq), lambda i, *_: (0, i)),
            ),
            scratch_shapes=[pltpu.VMEM((width, rows), jnp.bfloat16)],
        ),
        cost_estimate=pl.CostEstimate(
            flops=16 * heads * rows * rows * HEAD, transcendentals=heads * rows * rows, bytes_accessed=10 * rows * width
        ),
        name="attend",
    )(lo, hi, qkv, qkv, qkv, seg[None, :], seg[:, None])


def attend_back_kernel(
    lo_ref, hi_ref, q_ref, do_ref, lse_ref, dot_ref, k_ref, v_ref, seg_q, seg_k,
    d_ref, dk_sum, dv_sum, kt_ref, *, bk, heads,
):
    i = pl.program_id(0)
    bq, width = q_ref.shape

    @pl.when(i == 0)
    def _():
        kt_ref[...] = k_ref[...].T
        dk_sum[...] = jnp.zeros_like(dk_sum)
        dv_sum[...] = jnp.zeros_like(dv_sum)

    def body(j, carry):
        ks = pl.ds(pl.multiple_of(j * bk, bk), bk)
        same = seg_k[ks, :] == seg_q[...]
        out, dks, dvs = [], [], []
        for h in range(heads):
            hs = slice(h * HEAD, (h + 1) * HEAD)
            qh = q_ref[:, hs]
            doh = do_ref[:, hs]
            s = dot32(k_ref[ks, hs], qh, NT)
            p = jnp.exp(jnp.where(same, s - lse_ref[h : h + 1, :], NEG_FILL))
            dp = dot32(v_ref[ks, hs], doh, NT)
            ds = (p * (dp - dot_ref[h : h + 1, :])).astype(jnp.bfloat16)
            dvs.append(dot32(p.astype(jnp.bfloat16), doh, NN))
            dks.append(dot32(ds, qh, NN))
            out.append(carry[h] + dot32(kt_ref[hs, ks], ds, NN))
        dk_sum[ks, :] += jnp.concatenate(dks, axis=1)
        dv_sum[ks, :] += jnp.concatenate(dvs, axis=1)
        return tuple(out)

    first = tuple(jnp.zeros((HEAD, bq), jnp.float32) for _ in range(heads))
    found = lax.fori_loop(lo_ref[i], hi_ref[i], body, first)
    d_ref[pl.ds(pl.multiple_of(i * bq, bq), bq), :width] = jnp.concatenate(found, axis=0).T.astype(d_ref.dtype)

    @pl.when(i == pl.num_programs(0) - 1)
    def _():
        d_ref[:, width : 2 * width] = dk_sum[...].astype(d_ref.dtype)
        d_ref[:, 2 * width :] = dv_sum[...].astype(d_ref.dtype)


def attend_back(qkv, group, d_out, lse, row_dot, seg, lo, hi, bq, bk):
    rows, width = d_out.shape
    heads = width // HEAD
    by_row = lambda i, *_: (i, 0)
    by_col = lambda i, *_: (0, i)
    return pl.pallas_call(
        functools.partial(attend_back_kernel, bk=bk, heads=heads),
        out_shape=jax.ShapeDtypeStruct((rows, 3 * width), jnp.bfloat16),
        grid_spec=pltpu.PrefetchScalarGridSpec(
            num_scalar_prefetch=2,
            grid=(rows // bq,),
            in_specs=[
                pl.BlockSpec((bq, width), lambda i, *_: (i, 3 * group)),
                pl.BlockSpec((bq, width), by_row),
                pl.BlockSpec((heads, bq), by_col),
                pl.BlockSpec((heads, bq), by_col),
                pl.BlockSpec((rows, width), lambda i, *_: (0, 3 * group + 1)),
                pl.BlockSpec((rows, width), lambda i, *_: (0, 3 * group + 2)),
                pl.BlockSpec((1, bq), by_col),
                pl.BlockSpec((rows, 1), lambda i, *_: (0, 0)),
            ],
            out_specs=pl.BlockSpec((rows, 3 * width), lambda i, *_: (0, 0)),
            scratch_shapes=[
                pltpu.VMEM((rows, width), jnp.float32),
                pltpu.VMEM((rows, width), jnp.float32),
                pltpu.VMEM((width, rows), jnp.bfloat16),
            ],
        ),
        cost_estimate=pl.CostEstimate(
            flops=40 * heads * rows * rows * HEAD, transcendentals=heads * rows * rows, bytes_accessed=16 * rows * width
        ),
        name="attend_back",
    )(lo, hi, qkv, d_out, lse, row_dot, qkv, qkv, seg[None, :], seg[:, None])


def key_blocks(seg, length, bq, bk):
    lo = jnp.sum(seg[None, :] < seg[::bq][:, None], axis=1)
    hi = jnp.minimum(jnp.sum(seg[None, :] <= seg[bq - 1 :: bq][:, None], axis=1), length)
    lo = lo // bk
    hi = (hi + bk - 1) // bk
    dead = jnp.arange(seg.shape[0] // bq) * bq >= length
    return lo.astype(jnp.int32), jnp.where(dead, lo, hi).astype(jnp.int32)


TN = (((0,), (0,)), ((), ()))
PIECES = 8


def feed_kernel(spots, *refs, slices):
    n_ref, g_ref = refs[:2]
    w_in = [refs[2 + 4 * s : 6 + 4 * s] for s in range(slices)]
    at = 2 + 4 * slices
    out_ref, dn_ref = refs[at : at + 2]
    d_out = [refs[at + 2 + 4 * s : at + 6 + 4 * s] for s in range(slices)]
    w_buf, d_buf, w_sem, d_sem = refs[at + 2 + 4 * slices :]
    step = pl.program_id(0)
    slot = lax.rem(step, 2)

    def pieces(arrays, s, buf, sem, outward):
        held = s % 2
        for p in range(PIECES):
            lanes = pl.ds(pl.multiple_of(spots[s * PIECES + p] * LANES, LANES), LANES)
            far = arrays[p // 2].at[p % 2]
            near = buf.at[held, :, :, lanes]
            src, dst = (near, far) if outward else (far, near)
            yield pltpu.make_async_copy(src, dst, sem.at[held])

    for s in range(slices):

        @pl.when(step == s)
        def _(s=s):
            if s == 0:
                for first in range(min(2, slices)):
                    for copy in pieces(w_in[first], first, w_buf, w_sem, False):
                        copy.start()
            for copy in pieces(w_in[s], s, w_buf, w_sem, False):
                copy.wait()

    @pl.when(step == 0)
    def _():
        out_ref[...] = jnp.zeros_like(out_ref)
        dn_ref[...] = jnp.zeros_like(dn_ref)

    n = n_ref[...]
    g = g_ref[...]
    gate = dot32(n, w_buf[slot, 0], NT)
    up = dot32(n, w_buf[slot, 1], NT)
    d_hidden = dot32(g, w_buf[slot, 2], NT)
    square = gate * gate
    bent = jnp.tanh(gate * (GELU_IN + (GELU_IN * GELU_CUBE) * square))
    half = 0.5 + 0.5 * bent
    lifted = gate * half
    slope = half + (0.5 * gate) * (1.0 - bent * bent) * (GELU_IN + (3.0 * GELU_IN * GELU_CUBE) * square)
    hidden = (lifted * up).astype(jnp.bfloat16)
    d_gate = (d_hidden * up * slope).astype(jnp.bfloat16)
    d_up = (d_hidden * lifted).astype(jnp.bfloat16)
    out_ref[...] += dot32(hidden, w_buf[slot, 2], NN)
    dn_ref[...] += dot32(d_gate, w_buf[slot, 0], NN) + dot32(d_up, w_buf[slot, 1], NN)

    for s in range(2, slices):

        @pl.when(step == s)
        def _(s=s):
            for copy in pieces(d_out[s - 2], s - 2, d_buf, d_sem, True):
                copy.wait()

    d_buf[slot, 2] = dot32(hidden, g, TN).astype(jnp.bfloat16)
    d_buf[slot, 0] = dot32(d_gate, n, TN).astype(jnp.bfloat16)
    d_buf[slot, 1] = dot32(d_up, n, TN).astype(jnp.bfloat16)

    for s in range(slices):

        @pl.when(step == s)
        def _(s=s):
            for copy in pieces(d_out[s], s, d_buf, d_sem, True):
                copy.start()
            if s + 2 < slices:
                for copy in pieces(w_in[s + 2], s + 2, w_buf, w_sem, False):
                    copy.start()
            if s == slices - 1:
                for last in range(max(0, slices - 2), slices):
                    for copy in pieces(d_out[last], last, d_buf, d_sem, True):
                        copy.wait()


def feed(n, g, weights, spots):
    slices = len(weights)
    rows, width = n.shape
    hidden = weights[0][0].shape[2]
    whole = pl.BlockSpec((rows, width), lambda i, *_: (0, 0))
    there = pl.BlockSpec(memory_space=pl.ANY)
    acc = jax.ShapeDtypeStruct((rows, width), jnp.float32)
    part = jax.ShapeDtypeStruct((2, 3, hidden, LANES), jnp.bfloat16)
    found = pl.pallas_call(
        functools.partial(feed_kernel, slices=slices),
        out_shape=(acc, acc) + (part,) * (4 * slices),
        grid_spec=pltpu.PrefetchScalarGridSpec(
            num_scalar_prefetch=1,
            grid=(slices,),
            in_specs=[whole, whole] + [there] * (4 * slices),
            out_specs=(whole, whole) + (there,) * (4 * slices),
            scratch_shapes=[
                pltpu.VMEM((2, 3, hidden, width), jnp.bfloat16),
                pltpu.VMEM((2, 3, hidden, width), jnp.bfloat16),
                pltpu.SemaphoreType.DMA((2,)),
                pltpu.SemaphoreType.DMA((2,)),
            ],
        ),
        cost_estimate=pl.CostEstimate(
            flops=27 * slices * rows * hidden * width,
            transcendentals=slices * rows * hidden,
            bytes_accessed=12 * slices * hidden * width + 12 * rows * width,
        ),
        name="feed",
    )(spots, n, g, *[array for slice_ in weights for array in slice_])
    return found[0], found[1], [found[2 + 4 * s : 6 + 4 * s] for s in range(slices)]


def swap_over(axis, count, bit):
    return [(i, i ^ bit) for i in range(count)]


def spots_of(me, chip_bits):
    rows = []
    for first, second in chip_bits:
        rows += [0, first, second, first | second, 1, 1 | first, 1 | second, 1 | first | second]
    return jnp.bitwise_xor(me, jnp.array(rows, jnp.int32))


def after(value, *others):
    return lax.optimization_barrier((value, *others))[0]


def place_kernel(spots, *refs, split, sets, high, outward):
    if outward:
        whole, pieces, sem = refs[0], refs[1:-1], refs[-1]
    else:
        pieces, whole, sem = refs[:-2], refs[-2], refs[-1]
    count = sum(split)
    copies = []
    k = 0
    for piece, size in zip(pieces, split):
        for j in range(size):
            for s in range(sets):
                lanes = pl.ds(pl.multiple_of(spots[k] * LANES, LANES), LANES)
                rows = pl.ds(pl.multiple_of(spots[count + s] * high, high), high)
                near, far = whole.at[rows, lanes], piece.at[j, s]
                src, dst = (near, far) if outward else (far, near)
                copies.append(pltpu.make_async_copy(src, dst, sem))
            k += 1
    for copy in copies:
        copy.start()
    for copy in copies:
        copy.wait()


def join(pieces, spots):
    split = tuple(piece.shape[0] for piece in pieces)
    _, sets, high, _ = pieces[0].shape
    shape = (sets * high, sum(split) * LANES)
    return pl.pallas_call(
        functools.partial(place_kernel, split=split, sets=sets, high=high, outward=False),
        out_shape=jax.ShapeDtypeStruct(shape, pieces[0].dtype),
        grid_spec=pltpu.PrefetchScalarGridSpec(
            num_scalar_prefetch=1,
            grid=(1,),
            in_specs=[pl.BlockSpec(memory_space=pl.ANY)] * len(pieces),
            out_specs=pl.BlockSpec(shape, lambda i, *_: (0, 0)),
            scratch_shapes=[pltpu.SemaphoreType.DMA],
        ),
        name="join",
    )(spots, *pieces)


def part(whole, spots, split, sets):
    high = whole.shape[0] // sets
    there = pl.BlockSpec(memory_space=pl.ANY)
    return pl.pallas_call(
        functools.partial(place_kernel, split=split, sets=sets, high=high, outward=True),
        out_shape=tuple(jax.ShapeDtypeStruct((size, sets, high, LANES), whole.dtype) for size in split),
        grid_spec=pltpu.PrefetchScalarGridSpec(
            num_scalar_prefetch=1,
            grid=(1,),
            in_specs=[pl.BlockSpec(whole.shape, lambda i, *_: (0, 0))],
            out_specs=(there,) * len(split),
            scratch_shapes=[pltpu.SemaphoreType.DMA],
        ),
        name="part",
    )(spots, whole)


def on_device(
    inputs, cotangent, segment_ids, row_length,
    w_qkv, m_qkv, v_qkv, w_out, m_out, v_out, w_gate_up, m_gate_up, v_gate_up, w_down, m_down, v_down,
    norm_gains, m_gains, v_gains,
    *, dp, mp,
):
    f32, bf16 = jnp.float32, jnp.bfloat16
    low = lambda value: value.astype(bf16)
    wide_of = lambda value: value.astype(f32)
    z = lax.axis_index("mp")
    me = lax.axis_index("dp")
    core = lax.rem(me, 2)
    rows, width = inputs.shape[1:]
    seq_len = segment_ids.shape[1]
    hidden_here = w_down.shape[0]
    lanes_here = w_down.shape[1]
    heads_width = w_out.shape[0]
    exchange = dp == PIECES and lanes_here == LANES
    parts_of_heads = 2
    share = heads_width // parts_of_heads

    swap = lambda value, bit: lax.ppermute(value, "dp", swap_over("dp", dp, bit))
    pair = lambda value: swap(value, 1)
    line = lambda value, pairs: lax.ppermute(value, "mp", pairs)
    onward = lambda value: line(value, [(i, (i + 1) % mp) for i in range(mp)])
    backward = lambda value: line(value, [(i, (i - 1) % mp) for i in range(mp)])
    across = lambda value: line(value, swap_over("mp", mp, 2))
    tie = lambda *values: lax.optimization_barrier(values)

    def toward(value, first_row, back=False):
        pairs = []
        for d in range(dp):
            for a, b in first_row:
                a, b = (a, b) if d % 2 == 0 else (mp - 1 - a, mp - 1 - b)
                pairs.append((d * mp + b, d * mp + a) if back else (d * mp + a, d * mp + b))
        return lax.ppermute(value, ("dp", "mp"), pairs)

    home = z // 2
    at_home = home == core
    first = core == 0
    edge = (z == 0) | (z == mp - 1)
    mirrored = jnp.where(home == 0, z, mp - 1 - z)
    at_edge = at_home & edge
    steps = ([(3, 2), (2, 1), (1, 0)], [(2, 1), (1, 0)], [(1, 0), (0, 1)])

    copy_qkv = low(w_qkv).reshape(3, lanes_here, parts_of_heads, share).transpose(2, 0, 3, 1)
    copy_qkv = copy_qkv.reshape(3 * heads_width, lanes_here)
    copy_first = jnp.concatenate([copy_qkv, jnp.pad(low(norm_gains), ((0, 14), (0, 0)))])
    copy_out = low(w_out)
    copy_feed = jnp.concatenate([low(w_gate_up).transpose(0, 2, 1), low(w_down)[None]])
    chip_bits = [(2, 4), (4, 2), (4, 2), (2, 4)] if exchange else [(2, 4)] * mp
    spots = spots_of(me if exchange else 0, chip_bits).reshape(mp, PIECES)

    x_own = inputs[0]
    x_one = toward(x_own, steps[0])
    far_first = across(copy_first)
    ids = jnp.concatenate([segment_ids[0], jnp.broadcast_to(row_length, (LANES,))])
    ids = jnp.where(at_home, ids, pair(ids))
    x_two = toward(x_one, steps[1])
    x_far = toward(jnp.where(at_edge, x_own, x_two), steps[2])
    blocks = [mirrored, mirrored + 1, jnp.where(edge, 2, 3), jnp.where(edge, 3, 0)]
    blocks = [jnp.where(home == 0, block, mp - 1 - block) for block in blocks]

    if exchange:
        own_first = jnp.where(first, copy_first, far_first)
        two = jnp.stack([own_first, pair(jnp.where(first, far_first, copy_first))])
        by_x, by_y = swap(two, 2), swap(two, 4)
        corner = [swap(by_x[:1], 4), swap(by_y[1:], 2)]
        spots_first = jnp.concatenate([me ^ jnp.arange(PIECES, dtype=jnp.int32), jnp.zeros((1,), jnp.int32)])
        full_first = join([value[:, None] for value in (two, by_x, by_y, *corner)], spots_first)
    else:
        full_first = lax.all_gather(jnp.stack([copy_first, far_first]), "dp", axis=2, tiled=True)
        full_first = jnp.where(first, full_first[0], full_first[1])
    full_qkv = full_first[: 3 * heads_width]
    gain_one = wide_of(full_first[3 * heads_width])
    gain_two = wide_of(full_first[3 * heads_width + 1])

    seg_row = ids[:seq_len]
    length = ids[seq_len]
    live_row = jnp.arange(seq_len, dtype=jnp.int32) < length
    live = wide_of(live_row)[:, None]
    wide, narrow = min(1024, seq_len), min(512, seq_len)
    lo, hi = key_blocks(seg_row, length, wide, narrow)
    lo_back, hi_back = key_blocks(seg_row, length, narrow, narrow)

    def hop_one(piece, s):
        return jnp.stack([piece, swap(piece, chip_bits[s][0])]) if exchange else piece

    def hop_two(found, s):
        return swap(found, chip_bits[s][1]) if exchange else found

    def hop_core(found, other, s):
        if exchange:
            return [found, other, pair(found), pair(other)]
        whole = lax.all_gather(found, "dp", axis=2, tiled=True)
        whole = whole.reshape(3, hidden_here, PIECES, LANES)
        whole = [whole[:, :, block] for block in (0, 2, 4, 6, 1, 3, 5, 7)]
        return [jnp.stack(whole[2 * i : 2 * i + 2]) for i in range(4)]

    copy_late = after(copy_feed, by_x, by_y) if exchange else copy_feed
    near_zero = hop_one(copy_late, 0)
    if exchange:
        out_one = onward(copy_out)
        out_all = jnp.stack([copy_out, out_one, onward(out_one), backward(copy_out)])[None]

    hats = []
    normed_one = jnp.zeros((seq_len, width), bf16)
    for value, block in zip((x_own, x_one, x_two, x_far), blocks):
        piece = wide_of(jnp.where(at_home, value, pair(value)))
        hats.append(piece * rms_scale(piece))
        normed_one = lax.dynamic_update_slice(normed_one, low(hats[-1] * gain_one), (block * rows, 0))
    qkv = low(dot32(normed_one, full_qkv, NT))

    rank = 2 * lax.rem(z, 2) + core

    def column_pairs(s):
        found = []
        for d in range(dp):
            for c in range(mp):
                to_dp = (d // 2) * 2 + c // 2
                to_z = (2 * (c % 2) + d % 2) ^ s
                found.append((d * mp + c, to_dp * mp + to_z))
        return found

    def spread(value):
        return [
            lax.ppermute(lax.dynamic_slice(value, ((rank ^ s) * rows, 0), (rows, share)), ("dp", "mp"), column_pairs(s))
            for s in range(mp)
        ]

    def collect(value, i):
        found = []
        for s in range(mp):
            piece = value[:, s * heads_width + i * share : s * heads_width + (i + 1) * share]
            found.append(lax.ppermute(piece, ("dp", "mp"), [(there, here) for here, there in column_pairs(s)]))
        return found

    def in_row_order(found):
        found = jnp.stack(found)
        return jnp.concatenate([lax.dynamic_index_in_dim(found, rank ^ block, 0, False) for block in range(mp)])

    feed_in = after(copy_feed, x_far)
    plus, minus = onward(feed_in), backward(feed_in)
    far_zero = hop_two(near_zero, 0)
    out_x = swap(out_all, 2) if exchange else copy_out
    raw_one, logs_one = attend(qkv, 0, share, seg_row, lo, hi, wide, narrow)
    raw_one, logs_one, plus, minus, far_zero, out_x, qkv_next = tie(raw_one, logs_one, plus, minus, far_zero, out_x, qkv)
    twice = onward(plus)
    near_plus, near_minus = hop_one(plus, 1), hop_one(minus, 3)
    spread_one = spread(low(raw_one * live))
    feed_zero = hop_core(near_zero, far_zero, 0)
    if exchange:
        out_two = jnp.concatenate([out_all, out_x])
        out_y = swap(out_two, 4)
    else:
        out_y = out_x
    raw_two, logs_two = attend(qkv_next, 1, share, seg_row, lo, hi, wide, narrow)
    raw_two, logs_two, twice, near_plus, near_minus, out_y, *spread_one = tie(
        raw_two, logs_two, twice, near_plus, near_minus, out_y, *spread_one
    )
    spread_two = spread(low(raw_two * live))
    far_plus = hop_two(near_plus, 1)
    near_twice = hop_one(twice, 2)
    far_minus = hop_two(near_minus, 3)
    raw_out = [raw_one, raw_two]
    log_sums = [jnp.where(live_row[None, :], logs, -NEG_FILL) for logs in (logs_one, logs_two)]

    places = jnp.arange(mp, dtype=jnp.int32)
    group_place = lambda group: (2 * lax.rem(group, 2) + (core ^ (group // 2))) ^ z
    if exchange:
        spots_out = jnp.concatenate([
            me ^ jnp.array([0, 2, 4, 6, 1, 3, 5, 7], jnp.int32), group_place(lax.rem(z + mp - places, mp))
        ])
        out_four = jnp.concatenate([out_two, out_y])
        full_out = join([out_four, pair(out_four)], spots_out)
    else:
        place = z ^ places
        groups_here = (2 * core + place // 2) ^ (2 * lax.rem(place, 2))
        full_out = lax.all_gather(copy_out, ("dp", "mp"), axis=0)
        full_out = full_out.reshape(dp, mp, heads_width, lanes_here).transpose(1, 2, 0, 3)[groups_here]
        full_out = full_out.reshape(mp * heads_width, width)

    attended = jnp.concatenate([spread_one[s // 2] if s % 2 == 0 else spread_two[s // 2] for s in range(2 * mp)], axis=1)
    resid_in = wide_of(x_own)
    after_attn = resid_in + dot32(attended, full_out, NN)
    scale_two = rms_scale(after_attn)
    hat_two = after_attn * scale_two
    normed_two = low(hat_two * gain_two)

    spots_one = jnp.concatenate([spots[0], spots[1]])
    spots_two = jnp.concatenate([spots[3], spots[2]])
    feed_one = [feed_zero, hop_core(near_plus, far_plus, 1)]
    normed_two, far_minus, near_twice = tie(normed_two, far_minus, near_twice)
    far_twice = hop_two(near_twice, 2)
    feed_minus = hop_core(near_minus, far_minus, 3)
    fed_one, back_one, grads_one = feed(normed_two, cotangent[0], feed_one, spots_one)
    fed_one, back_one, far_twice, *feed_minus = tie(fed_one, back_one, far_twice, *feed_minus)
    feed_two = [feed_minus, hop_core(near_twice, far_twice, 2)]
    held = [pair(grads[k]) for grads in grads_one for k in (3, 2)] if exchange else []
    fed_two, back_two, grads_two = feed(normed_two, cotangent[0], feed_two, spots_two)
    if exchange:
        fed_two, back_two, *held = tie(fed_two, back_two, *held)
        away = [low(wide_of(grads_one[i][1]) + wide_of(held[2 * i])) for i in range(2)]
        near = [wide_of(grads_one[i][0]) + wide_of(held[2 * i + 1]) for i in range(2)]
        away = [swap(away[i], chip_bits[(0, 1)[i]][1]) for i in range(2)]
        held = [pair(grads[k]) for grads in grads_two for k in (3, 2)]

    d_normed_two = back_one + back_two
    d_after = wide_of(cotangent[0]) + norm_back(d_normed_two, hat_two, scale_two, gain_two)
    d_branch = low(d_after)
    d_attended = low(dot32(d_branch, full_out, NT))
    d_first = collect(d_attended, 0)
    d_second = collect(d_attended, 1)
    grad_out = low(dot32(attended, d_branch, TN))

    def heads_back(found, i):
        d_here = jnp.where(live_row[:, None], in_row_order(found), jnp.zeros((), bf16))
        row_dot = jnp.sum((raw_out[i] * d_here).reshape(seq_len, share // HEAD, HEAD), axis=-1).T
        return d_here, row_dot

    d_here, row_dot = heads_back(d_first, 0)
    if exchange:
        out_near, out_core = part(grad_out, spots_out, (4, 4), mp)
        d_here, row_dot, out_near, out_core, *away = tie(d_here, row_dot, out_near, out_core, *away)
        near = [near[i] + wide_of(away[i]) for i in range(2)]
        ends = [swap(low(near[i][1]), chip_bits[(0, 1)[i]][0]) for i in range(2)]
        away = [low(wide_of(grads_two[i][1]) + wide_of(held[2 * i])) for i in range(2)]
        near_two = [wide_of(grads_two[i][0]) + wide_of(held[2 * i + 1]) for i in range(2)]
        away = [swap(away[i], chip_bits[(3, 2)[i]][1]) for i in range(2)]
        out_core = pair(out_core)
    d_qkv_one = attend_back(qkv, 0, d_here, log_sums[0], row_dot, seg_row, lo_back, hi_back, narrow, narrow)
    d_here, row_dot = heads_back(d_second, 1)
    if exchange:
        d_qkv_one, d_here, out_core, *found = tie(d_qkv_one, d_here, out_core, *ends, *away)
        owned = [near[i][0] + wide_of(found[i]) for i in range(2)]
        near_two = [near_two[i] + wide_of(found[2 + i]) for i in range(2)]
        ends = [swap(low(near_two[i][1]), chip_bits[(3, 2)[i]][0]) for i in range(2)]
        from_one = backward(low(owned[1]))
        out_near = wide_of(out_near) + wide_of(out_core)
        out_away = swap(low(out_near[2:]), 4)
    d_qkv_two = attend_back(qkv, 1, d_here, log_sums[1], row_dot, seg_row, lo_back, hi_back, narrow, narrow)
    if exchange:
        d_qkv_two, from_one, out_away, *ends = tie(d_qkv_two, from_one, out_away, *ends)
    d_qkv = jnp.concatenate([d_qkv_one, d_qkv_two], axis=1)
    block_output = after_attn + (fed_one + fed_two)
    grad_gain_two = jnp.sum(d_normed_two * hat_two, axis=0)

    grad_gain_one = jnp.zeros((width,), f32)
    sums = [None] * mp
    for k in range(mp - 1, -1, -1):
        found = dot32(lax.dynamic_slice(d_qkv, (blocks[k] * rows, 0), (rows, d_qkv.shape[1])), full_qkv, NN)
        grad_gain_one = grad_gain_one + jnp.sum(found * hats[k], axis=0)
        sums[k] = jnp.where(at_home, found + wide_of(pair(low(found))), 0.0)
    inward = wide_of(toward(low(sums[3]), steps[2], back=True))
    inward_two = toward(low(jnp.where(at_edge, sums[2], sums[2] + inward)), steps[1], back=True)
    inward_one = toward(low(sums[1] + wide_of(inward_two)), steps[0], back=True)
    d_normed_one = jnp.where(at_edge, sums[0] + inward, sums[0]) + wide_of(inward_one)
    scale_one = rms_scale(resid_in)
    input_grad = d_after + norm_back(d_normed_one, resid_in * scale_one, scale_one, gain_one)

    grad_qkv = low(dot32(d_qkv, normed_one, TN))
    if exchange:
        near, far = part(grad_qkv, spots_first, (4, 4), 1)
        near = wide_of(near) + wide_of(swap(far, 4))
        near = near[:2] + wide_of(swap(low(near[2:]), 2))
        moved = wide_of(pair(low(near[1, 0])))
        here = jnp.where(first, near[0, 0], moved)
        there = jnp.where(first, moved, near[0, 0])
    else:
        nothing = jnp.zeros_like(grad_qkv)
        both = jnp.stack([jnp.where(first, grad_qkv, nothing), jnp.where(first, nothing, grad_qkv)])
        both = wide_of(lax.psum_scatter(both, "dp", scatter_dimension=2, tiled=True))
        here, there = both[0], both[1]
    grad_qkv = here + wide_of(across(low(there)))
    grad_qkv = grad_qkv.reshape(parts_of_heads, 3, share, lanes_here).transpose(1, 3, 0, 2).reshape(w_qkv.shape)

    if exchange:
        owned += [near_two[i][0] + wide_of(ends[i]) for i in range(2)]
        total = owned[0] + wide_of(from_one)
        total = total + wide_of(onward(low(owned[2] + wide_of(onward(low(owned[3]))))))
        out_near = out_near[:2] + wide_of(out_away)
        out_owned = out_near[0] + wide_of(swap(low(out_near[1]), 2))
        grad_out = wide_of(onward(low(wide_of(onward(low(out_owned[2]))) + out_owned[3])))
        grad_out = grad_out + wide_of(backward(low(out_owned[1]))) + out_owned[0]
    else:
        total = 0.0
        back = jnp.array([0, 4, 1, 5, 2, 6, 3, 7])
        for s, pieces in zip((0, 1, 3, 2), grads_one + grads_two):
            whole = jnp.concatenate(pieces)[back].transpose(1, 2, 0, 3).reshape(3, hidden_here, width)
            whole = lax.psum_scatter(whole, "dp", scatter_dimension=2, tiled=True)
            for _ in range(s):
                whole = backward(whole)
            total = total + wide_of(whole)
        grad_out = grad_out.reshape(mp, heads_width, width)[group_place(places)].reshape(mp * heads_width, width)
        grad_out = lax.psum_scatter(grad_out, "dp", scatter_dimension=1, tiled=True)
        grad_out = wide_of(lax.psum_scatter(grad_out, "mp", scatter_dimension=0, tiled=True))
    grad_gate_up = total[:2].transpose(0, 2, 1)
    grad_down = total[2]

    grad_gains = jnp.stack([grad_gain_one, grad_gain_two])
    for axis, count in (("mp", mp), ("dp", dp)):
        bit = 1
        while bit < count:
            grad_gains = grad_gains + lax.ppermute(grad_gains, axis, swap_over(axis, count, bit))
            bit *= 2
    grad_gains = lax.dynamic_slice(grad_gains, (0, me * lanes_here), (2, lanes_here))

    new_qkv = adam_update(w_qkv, m_qkv, v_qkv, grad_qkv, RATES[0], DECAY_RATE)
    new_out = adam_update(w_out, m_out, v_out, grad_out, RATES[1], DECAY_RATE)
    new_gate_up = adam_update(w_gate_up, m_gate_up, v_gate_up, grad_gate_up, RATES[2], DECAY_RATE)
    new_down = adam_update(w_down, m_down, v_down, grad_down, RATES[3], DECAY_RATE)
    new_gains = adam_update(norm_gains, m_gains, v_gains, grad_gains, RATES[4], 0.0)
    return (block_output[None], input_grad[None], *new_qkv, *new_out, *new_gate_up, *new_down, *new_gains)


def solution(mesh):
    tokens = P("dp", "mp", None)
    stacked = P(None, "dp", "mp")
    flat = P("mp", "dp")
    gains = P(None, "dp")
    return jax.shard_map(
        functools.partial(on_device, dp=mesh.shape["dp"], mp=mesh.shape["mp"]),
        mesh=mesh,
        in_specs=(tokens, tokens, P("dp", None), P("dp"))
        + (stacked,) * 3 + (flat,) * 3 + (stacked,) * 3 + (flat,) * 3 + (gains,) * 3,
        out_specs=(tokens, tokens) + (stacked,) * 4 + (flat,) * 4 + (stacked,) * 4 + (flat,) * 4 + (gains,) * 4,
        check_vma=False,
    )
```
